32 devices in a mesh: group: 8 (over z, x), space: 4 (over y, core).
Axes of the slice: x: 2, y: 2, z: 4, core: 2. Of those that a mesh axis runs over, the one named last changes fastest.
Arguments:
- latent: bfloat16 [16384, 128], P(('group', 'space')), may hold values from -6 to 6
- owner_ids: int32 [16384, 1], P(('group', 'space')), may hold values from 0 to 7; in each aligned block of 512 rows (0 to 511, 512 to 1023, ...) at most 160 rows name the same one
- tile_recv: int32 [2048], P(('group', 'space')), may hold values from 0 to 3
- tile_send: int32 [2048], P(('group', 'space')), may hold values from 0 to 15
- kernels: bfloat16 [2048, 128, 128], P(('group', 'space')), may hold values from -0.125 to 0.125
- w_msg: bfloat16 [128, 128], replicated, may hold values from -0.5 to 0.5
- w_node: bfloat16 [256, 128], replicated, may hold values from -0.375 to 0.375
- upstream: bfloat16 [40960, 128], P(('group', 'space')), may hold values from -6 to 6
Outputs:
- updated: bfloat16 [40960, 128], P(('group', 'space'))
- latent_grad: bfloat16 [16384, 128], P(('group', 'space'))
- grad_msg: float32 [128, 128], replicated
- grad_node: float32 [256, 128], replicated
The draws below stay inside these ranges and needn't reach their ends.
Inputs may be any that keep to these rules, and one draw needn't show every extreme that they name: `owner_ids`: in the particles of one device no owner is named more than 160 times; in some devices one owner is named exactly 160 times.
All inputs are finite; a program needn't handle non-finite values.
Results may differ from the reference program's by a relative error of at most 0.022.
Values may be sent and summed in bfloat16 or wider, within the bound.
No kernel may reach another device: no remote copies, remote signals or barrier semaphores. Data moves between devices by JAX's collectives and lax.ppermute only.
A program may use at most 64 MiB of HBM per device.

```python
import math
import jax
import jax.numpy as jnp
import numpy as np
from jax import lax

H = 128
BLOCK = 128
NODE_DEV = 512
TILE_DEV = 64
CAP = 160
SLOTS = 1280
NODES = 16384
TILES = 2048
N_GROUP = 8
N_SPACE = 4
DEVICES = 32


def plant(result, own_key, low, high):
    longest = result.shape.index(max(result.shape))
    spots = []
    for shift in (0, 1):
        where = [jax.random.randint(jax.random.fold_in(own_key, axis), (), 0, length) for axis, length in enumerate(result.shape)]
        where[longest] = (where[longest] + shift) % result.shape[longest]
        spots.append(tuple(where))
    return result.at[spots[0]].set(low).at[spots[1]].set(high)


def shard_levels(stream_key, extent, shards, least, top_value):
    factor_of = 1.0
    for axis_at, blocks in shards:
        draws = jax.random.uniform(jax.random.fold_in(jax.random.fold_in(stream_key, 6), axis_at), (blocks,), jnp.float32, least / len(shards), top_value / len(shards))
        factor_of = factor_of * jnp.repeat(jnp.exp(draws), extent[axis_at] // blocks).reshape((-1,) + (1,) * (len(extent) - 1 - axis_at))
    return factor_of


def routed_block(stream_key, own, number, rows, number_of, top, most, skew):
    ranking = jax.random.permutation(stream_key, number_of)
    packed, usual = portions_of(number_of, rows * top, most, skew, True), portions_of(number_of, rows * top, most, skew, False)
    places = jnp.arange(number_of)

    def named(sizes, rotation):
        used = int((sizes > 0).sum())
        fixed = max(1, used // 4)
        moved = fixed + (places - fixed + rotation * (used - fixed)) % max(1, number_of - fixed)
        return jnp.zeros((number_of,), jnp.int32).at[ranking[jnp.where(places < fixed, places, moved)]].set(jnp.asarray(sizes, jnp.int32))

    sizes = jnp.where(number % 4 == 0, named(packed, number // 4), named(usual, number - number // 4 - 1))
    mixed = jax.random.permutation(jax.random.fold_in(own, 3), number_of)
    source_of, sink = mixed[0:number_of // 2 * 2:2], mixed[1:number_of // 2 * 2:2]
    room = jnp.minimum(sizes[source_of] - 1, most - sizes[sink]) // 2
    room = jnp.where((source_of == ranking[0]) | (sink == ranking[0]) | (sizes[sink] == 0), 0, jnp.maximum(room, 0))
    moved = jax.random.randint(jax.random.fold_in(own, 4), (number_of // 2,), 0, 1 << 20) % (room + 1)
    sizes = sizes.at[source_of].add(-moved).at[sink].add(moved)
    items = jnp.searchsorted(jnp.cumsum(sizes), jnp.arange(rows * top), side="right").astype(jnp.int32)
    listing = items.reshape(top, rows).T
    listing = listing[jax.random.permutation(jax.random.fold_in(own, 1), rows)]
    rotation = jax.random.randint(jax.random.fold_in(own, 2), (rows, 1), 0, top)
    return jnp.take_along_axis(listing, (jnp.arange(top)[None, :] + rotation) % top, axis=1)


def portions_of(count, total, bound, lean, full):
    portions = [(1 << 20) // math.isqrt(grade ** lean) + 1 for grade in range(1, count + 1)]
    largest = bound if full else min(bound, max(-(-total // count), total * portions[0] // sum(portions)))
    least = 1 if total - largest >= count - 1 else 0
    counts, rest = [largest] + [least] * (count - 1), total - largest - least * (count - 1)
    while rest > 0:
        candidates = [i for i in range(1, count) if counts[i] < largest] or [i for i in range(1, count) if counts[i] < bound]
        whole, remaining = sum([portions[i] for i in candidates]), rest
        for i in candidates:
            more = min(bound - counts[i], max(1, remaining * portions[i] // whole), rest)
            counts[i] = counts[i] + more
            rest = rest - more
    return np.array(counts)


def scatter_about(stream_key, extent, scale, bound, split=(), held_as=jnp.bfloat16):
    values = jax.random.normal(stream_key, extent, jnp.float32) * scale
    if len(split) > 0:
        values = shard_levels(stream_key, extent, split, -0.22, 0.18) * values
    return jnp.clip(values, min=-bound, max=bound).astype(held_as)


def setup_inputs(seed: int = 0) -> dict:
    seeds = jax.random.split(jax.random.key(seed), 9)
    latent = scatter_about(seeds[0], (NODES, H), 1.0, 6.0, ((0, 32),))
    owner_ids_keys = jax.random.split(jax.random.fold_in(seeds[1], 1), NODES // NODE_DEV)
    owner_ids_turns = jax.random.permutation(jax.random.fold_in(seeds[1], 3), NODES // NODE_DEV)
    owner_ids = jax.vmap(lambda own, number: routed_block(jax.random.fold_in(seeds[1], 2), own, number, NODE_DEV, N_GROUP, 1, CAP, 1))(owner_ids_keys, owner_ids_turns).reshape((NODES, 1))
    tile_recv = plant(jax.random.randint(seeds[2], (TILES,), 0, NODE_DEV // BLOCK), jax.random.fold_in(seeds[2], 1), 0, (NODE_DEV // BLOCK) - 1).astype(jnp.int32)
    tile_send = plant(jax.random.randint(seeds[3], (TILES,), 0, N_SPACE * NODE_DEV // BLOCK), jax.random.fold_in(seeds[3], 1), 0, (N_SPACE * NODE_DEV // BLOCK) - 1).astype(jnp.int32)
    kernels = scatter_about(seeds[4], (TILES, BLOCK, BLOCK), (BLOCK * TILE_DEV // (NODE_DEV // BLOCK)) ** -0.5, 0.125, ((0, 32),))
    w_msg = scatter_about(seeds[5], (H, H), H ** -0.5, 0.5)
    w_node = scatter_about(seeds[6], (2 * H, H), (2 * H) ** -0.5, 0.375)
    upstream = scatter_about(seeds[7], (DEVICES * SLOTS, H), 1.0, 6.0, ((0, 32),))
    return {"latent": latent, "owner_ids": owner_ids, "tile_recv": tile_recv, "tile_send": tile_send, "kernels": kernels, "w_msg": w_msg, "w_node": w_node, "upstream": upstream}


def silu_slope(value):
    sigmoid_val = jax.nn.sigmoid(value)
    return sigmoid_val * (1.0 + value * (1.0 - sigmoid_val))


def contract_rows(left, right):
    return lax.dot_general(left, right, (((0,), (0,)), ((), ())), preferred_element_type=jnp.float32)


def times_transposed(left, right):
    return lax.dot_general(left, right, (((1,), (1,)), ((), ())), preferred_element_type=jnp.float32)


def reference(latent, owner_ids, tile_recv, tile_send, kernels, w_msg, w_node, upstream):
    preact = jnp.dot(latent, w_msg, preferred_element_type=jnp.float32)
    message = jax.nn.silu(preact).astype(jnp.bfloat16)
    per_group = N_SPACE * NODE_DEV
    recv_all = tile_recv.reshape(DEVICES, TILE_DEV)
    send_all = tile_send.reshape(DEVICES, TILE_DEV)
    kern_all = kernels.reshape(DEVICES, TILE_DEV, BLOCK, BLOCK)
    devices = jnp.arange(DEVICES, dtype=jnp.int32)

    def aggregate_one(inputs_one):
        device, receivers, sender_ids, kernel_set = inputs_one
        offset = ((device // N_SPACE) * per_group).astype(jnp.int32)
        ghost_table = lax.dynamic_slice_in_dim(message, offset, per_group, 0).reshape(-1, BLOCK, H)
        senders = ghost_table[sender_ids]
        products = jnp.einsum("tij,tjh->tih", kernel_set.astype(jnp.float32), senders.astype(jnp.float32))
        summed = jnp.zeros((NODE_DEV // BLOCK, BLOCK, H), jnp.float32).at[receivers].add(products)
        return summed.reshape(NODE_DEV, H).astype(jnp.bfloat16)

    aggregate = lax.map(aggregate_one, (devices, recv_all, send_all, kern_all)).reshape(NODES, H)
    joined = jnp.concatenate([latent, aggregate], axis=1)
    mixed = jnp.dot(joined, w_node, preferred_element_type=jnp.float32)
    new_rows = (latent.astype(jnp.float32) + jax.nn.silu(mixed)).astype(jnp.bfloat16)

    owner_col = owner_ids[:, 0].reshape(DEVICES, NODE_DEV)
    onehot = (owner_col[:, :, None] == jnp.arange(N_GROUP, dtype=jnp.int32)[None, None, :]).astype(jnp.int32)
    slot_rank = jnp.sum((jnp.cumsum(onehot, axis=1) - onehot) * onehot, axis=2)
    device_col = devices[:, None]
    slot_index = (((owner_col * N_SPACE + device_col % N_SPACE) * N_GROUP + device_col // N_SPACE) * CAP + slot_rank).reshape(NODES)
    updated = jnp.zeros((DEVICES * SLOTS, H), jnp.bfloat16).at[slot_index].set(new_rows)

    incoming = upstream[slot_index]
    slope = (incoming.astype(jnp.float32) * silu_slope(mixed)).astype(jnp.bfloat16)
    grad_node = contract_rows(joined, slope)
    padded_in = jnp.concatenate([incoming.astype(jnp.float32), jnp.zeros((NODES, H), jnp.float32)], axis=1)
    row_grad = (times_transposed(slope, w_node) + padded_in).astype(jnp.bfloat16)
    agg_grad = row_grad[:, H:].reshape(DEVICES, NODE_DEV, H)

    def spread_step(running, inputs_one):
        device, receivers, sender_ids, kernel_set, grad_rows = inputs_one
        blocks = grad_rows.reshape(-1, BLOCK, H)[receivers]
        spread = jnp.einsum("tij,tih->tjh", kernel_set.astype(jnp.float32), blocks.astype(jnp.float32))
        partial_sum = jnp.zeros((per_group // BLOCK, BLOCK, H), jnp.float32).at[sender_ids].add(spread)
        partial_sum = lax.optimization_barrier(partial_sum.reshape(per_group, H).astype(jnp.bfloat16)).astype(jnp.float32)
        offset = ((device // N_SPACE) * per_group).astype(jnp.int32)
        current = lax.dynamic_slice_in_dim(running, offset, per_group, 0)
        return lax.dynamic_update_slice_in_dim(running, current + partial_sum, offset, 0), None

    message_grad, _ = lax.scan(spread_step, jnp.zeros((NODES, H), jnp.float32), (devices, recv_all, send_all, kern_all, agg_grad))
    preact_grad = (message_grad * silu_slope(preact)).astype(jnp.bfloat16)
    grad_msg = contract_rows(latent, preact_grad)
    latent_grad = (times_transposed(preact_grad, w_msg) + row_grad[:, :H].astype(jnp.float32)).astype(jnp.bfloat16)
    return updated, latent_grad, grad_msg, grad_node
```

```python
import jax
import jax.numpy as jnp
from jax import lax
from jax.experimental import pallas as pl
from jax.experimental.pallas import tpu as pltpu
from jax.sharding import PartitionSpec as P

BF = jnp.bfloat16
F32 = jnp.float32


def mm(left, right):
    return jnp.dot(left, right, preferred_element_type=F32)


def mm_nt(left, right):
    return lax.dot_general(left, right, (((1,), (1,)), ((), ())), preferred_element_type=F32)


def sigmoid(value):
    return 0.5 * jnp.tanh(0.5 * value) + 0.5


def slope_of(value):
    sig = sigmoid(value)
    return sig * (1.0 + value * (1.0 - sig))


def make_layer(node_count, width, rows, tiles, groups, spaces, capacity):
    blocks = node_count // rows
    slots = groups * capacity
    group_rows = max(16, -(-groups // 16) * 16)

    def kernel(recv, send, owner, table, own_latent, kernels, w_msg, w_node, returned, *rest):
        outgoing = rest[0]
        parts = rest[1 : 1 + spaces]
        grads, direct_out = rest[1 + spaces : 3 + spaces]
        msg, acc, spread, place, place_t = rest[3 + spaces :]
        me = lax.axis_index("space")

        owner_row = owner[...]
        hot = (
            lax.broadcasted_iota(jnp.int32, (group_rows, node_count), 0) == owner_row
        ).astype(F32)
        before = (
            lax.broadcasted_iota(jnp.int32, (node_count, node_count), 0)
            < lax.broadcasted_iota(jnp.int32, (node_count, node_count), 1)
        ).astype(F32)
        counts = mm(hot.astype(BF), before.astype(BF))
        rank = jnp.sum(counts * hot, axis=0, keepdims=True)
        slot = owner_row.astype(F32) * capacity + rank
        slot_col = jnp.transpose(jnp.broadcast_to(slot, (width, node_count)))
        slot_int = slot.astype(jnp.int32)
        slot_col = slot_col.astype(jnp.int32)
        for at in range(0, slots, 128):
            down = lax.broadcasted_iota(jnp.int32, (128, node_count), 0) + at
            place[at : at + 128, :] = (down == slot_int).astype(F32).astype(BF)
            across = lax.broadcasted_iota(jnp.int32, (node_count, 128), 1) + at
            place_t[:, at : at + 128] = (across == slot_col).astype(F32).astype(BF)

        for part in range(spaces):
            preact = mm(table[part * node_count : (part + 1) * node_count, :], w_msg[...])
            value = (preact * sigmoid(preact)).astype(BF)
            for block in range(blocks):
                msg[part * blocks + block] = value[block * rows : (block + 1) * rows, :]

        acc[...] = jnp.zeros_like(acc)

        def gather_tile(t, carry):
            r = recv[t]
            acc[r] = acc[r] + mm(kernels[t], msg[send[t]])
            return carry

        lax.fori_loop(0, tiles, gather_tile, 0, unroll=8)
        aggregate = acc[...].reshape(node_count, width).astype(BF)
        latent = own_latent[...]
        joined = jnp.concatenate([latent, aggregate], axis=1)
        mixed = mm(joined, w_node[...])
        sig = sigmoid(mixed)
        new_rows = (latent.astype(F32) + mixed * sig).astype(BF)
        outgoing[...] = mm(place[...], new_rows).astype(BF)

        incoming = mm(place_t[...], returned[...])
        slope = incoming * (sig * (1.0 + mixed * (1.0 - sig)))
        slope_t = jnp.transpose(slope).astype(BF)
        slope = slope.astype(BF)
        grads[width : 3 * width, :] = jnp.transpose(mm(slope_t, joined)).astype(BF)
        direct_out[...] = (mm_nt(slope, w_node[0:width, :]) + incoming).astype(BF)
        back_t = mm(w_node[width : 2 * width, :], slope_t).astype(BF)
        for block in range(blocks):
            acc[block] = back_t[:, block * rows : (block + 1) * rows].astype(F32)

        spread[...] = jnp.zeros_like(spread)

        def spread_tile(t, carry):
            s = send[t]
            spread[s] = spread[s] + mm(acc[recv[t]].astype(BF), kernels[t])
            return carry

        lax.fori_loop(0, tiles, spread_tile, 0, unroll=8)

        w_msg_t = jnp.transpose(w_msg[...].astype(F32)).astype(BF)
        grad_msg = jnp.zeros((width, width), F32)
        for part in range(spaces):
            target = lax.rem(me + part, spaces)
            lat = table[pl.ds(pl.multiple_of(target * node_count, node_count), node_count), :]
            preact_t = mm_nt(w_msg_t, lat)
            total = jnp.concatenate(
                [spread[target * blocks + block] for block in range(blocks)], axis=1
            )
            preact_grad = (total * slope_of(preact_t)).astype(BF)
            grad_msg += mm(preact_grad, lat)
            parts[part][...] = mm(w_msg[...], preact_grad).astype(BF)
        grads[0:width, :] = jnp.transpose(grad_msg).astype(BF)

    vmem = pl.BlockSpec(memory_space=pltpu.VMEM)
    smem = pl.BlockSpec(memory_space=pltpu.SMEM)
    return pl.pallas_call(
        kernel,
        out_shape=(
            jax.ShapeDtypeStruct((slots, width), BF),
            *[jax.ShapeDtypeStruct((width, node_count), BF)] * spaces,
            jax.ShapeDtypeStruct((3 * width, width), BF),
            jax.ShapeDtypeStruct((node_count, width), BF),
        ),
        in_specs=[smem, smem] + [vmem] * 7,
        out_specs=[vmem] * (spaces + 3),
        scratch_shapes=[
            pltpu.VMEM((spaces * blocks, rows, width), BF),
            pltpu.VMEM((blocks, rows, width), F32),
            pltpu.VMEM((spaces * blocks, width, rows), F32),
            pltpu.VMEM((slots, node_count), BF),
            pltpu.VMEM((node_count, slots), BF),
        ],
        compiler_params=pltpu.CompilerParams(vmem_limit_bytes=40 << 20),
        cost_estimate=pl.CostEstimate(
            flops=2_000_000_000, bytes_accessed=4_000_000, transcendentals=600_000
        ),
        name="layer",
    )


def finish_kernel(direct, *rest):
    total = rest[0][...].astype(F32)
    for ref in rest[1:-1]:
        total = total + ref[...].astype(F32)
    rest[-1][...] = (jnp.transpose(total) + direct[...].astype(F32)).astype(BF)


def exchange(value, axes, size, mask):
    return lax.ppermute(value, axes, [(i, i ^ mask) for i in range(size)])


def sum_all(value, axes, size):
    bits = size.bit_length() - 1
    stages = [(0, 1)] + [(at, min(2, bits - at)) for at in range(1, bits, 2)]
    for at, span in stages:
        wide = value.astype(BF)
        got = [exchange(wide, axes, size, step << at) for step in range(1, 1 << span)]
        got = [wide.astype(F32)] + [one.astype(F32) for one in got]
        value = got[0] + got[1]
        if span == 2:
            value = value + (got[2] + got[3])
    return value


def body(latent, owner_ids, tile_recv, tile_send, kernels, w_msg, w_node, upstream):
    node_count, width = latent.shape
    tiles, rows, _ = kernels.shape
    groups, spaces = lax.axis_size("group"), lax.axis_size("space")
    slots = upstream.shape[0]
    capacity = slots // groups

    def swap(value):
        return lax.all_to_all(
            value.reshape(groups, capacity, width), "group", split_axis=0, concat_axis=0, tiled=True
        ).reshape(slots, width)

    returned = swap(upstream)
    table = lax.all_gather(latent, "space", axis=0, tiled=True)
    layer = make_layer(node_count, width, rows, tiles, groups, spaces, capacity)
    outs = layer(
        tile_recv, tile_send, owner_ids.reshape(1, node_count), table, latent, kernels, w_msg,
        w_node, returned,
    )
    outgoing, parts, grads, direct = outs[0], outs[1 : 1 + spaces], outs[-2], outs[-1]
    updated = swap(outgoing)
    got = [
        lax.ppermute(parts[k], "space", [(i, (i + k) % spaces) for i in range(spaces)])
        for k in range(1, spaces)
    ]
    total = sum_all(grads, ("group", "space"), groups * spaces)
    latent_grad = pl.pallas_call(
        finish_kernel, out_shape=jax.ShapeDtypeStruct((node_count, width), BF), name="finish"
    )(direct, parts[0], *got)
    return updated, latent_grad, total[:width], total[width:]


def solution(mesh):
    split = P(("group", "space"))
    wide = P(("group", "space"), None)
    return jax.shard_map(
        body,
        mesh=mesh,
        in_specs=(wide, wide, split, split, P(("group", "space"), None, None), P(), P(), wide),
        out_specs=(wide, wide, P(), P()),
        check_vma=False,
    )
```

```python
import jax
import jax.numpy as jnp
from jax import lax
from jax.experimental import pallas as pl
from jax.experimental.pallas import tpu as pltpu
from jax.sharding import PartitionSpec as P

BF = jnp.bfloat16
F32 = jnp.float32
VMEM = pl.BlockSpec(memory_space=pltpu.VMEM)
ANY = pl.BlockSpec(memory_space=pltpu.HBM)


def mm(left, right):
    return jnp.dot(left, right, preferred_element_type=F32)


def mm_nt(left, right):
    return lax.dot_general(left, right, (((1,), (1,)), ((), ())), preferred_element_type=F32)


def sigmoid(value):
    return 0.5 * jnp.tanh(0.5 * value) + 0.5


def slope_of(value):
    sig = sigmoid(value)
    return sig * (1.0 + value * (1.0 - sig))


def in_hbm(value):
    return pltpu.with_memory_space_constraint(value, pltpu.HBM)


def iota(shape, axis):
    return lax.broadcasted_iota(jnp.int32, shape, axis)


class Sizes:
    def __init__(self, latent, kernels, upstream):
        self.nodes, self.width = latent.shape
        self.tiles, self.rows, _ = kernels.shape
        self.groups, self.spaces = lax.axis_size("group"), lax.axis_size("space")
        self.slots = upstream.shape[0]
        self.capacity = self.slots // self.groups
        self.blocks = self.nodes // self.rows
        self.half = self.spaces // 2
        self.hot = max(16, -(-self.groups // 16) * 16)

    def place_of(self, sender):
        me = lax.axis_index("space")
        device = sender // self.blocks
        step = lax.rem((me >> 1) - (device >> 1) + self.half, self.half)
        other = (me & 1) ^ (device & 1)
        return (2 * step + other) * self.blocks + lax.rem(sender, self.blocks)


def forward_call(z):
    def kernel(recv_hbm, send_hbm, owner_hbm, kern_hbm, w_msg_hbm, w_node_hbm, lat_hbm, *rest):
        others, rest = rest[: z.spaces - 1], rest[z.spaces - 1 :]
        outgoing, slot_out, factor, agg, pre_slope = rest[:5]
        recv, send, owner, w_msg, w_node, kern, msg, acc, place, latent, sems = rest[5:]
        lats = (latent, *others)
        copies = [
            pltpu.make_async_copy(src, dst, sems.at[i])
            for i, (src, dst) in enumerate(
                [
                    (owner_hbm, owner),
                    (w_msg_hbm, w_msg),
                    (lat_hbm, latent),
                    (recv_hbm, recv),
                    (send_hbm, send),
                    (kern_hbm, kern),
                    (w_node_hbm, w_node),
                ]
            )
        ]
        for copy in copies:
            copy.start()
        copies[0].wait()

        owner_row = owner[...]
        hot = (iota((z.hot, z.nodes), 0) == owner_row).astype(F32)
        before = (iota((z.nodes, z.nodes), 0) < iota((z.nodes, z.nodes), 1)).astype(F32)
        counts = mm(hot.astype(BF), before.astype(BF))
        rank = jnp.sum(counts * hot, axis=0, keepdims=True)
        slot = owner_row.astype(F32) * z.capacity + rank
        slot_row = slot.astype(jnp.int32)
        slot_out[...] = slot
        for at in range(0, z.slots, 128):
            down = iota((128, z.nodes), 0) + at
            place[at : at + 128, :] = (down == slot_row).astype(F32).astype(BF)

        copies[1].wait()
        copies[2].wait()
        for part in range(z.spaces):
            preact = mm(lats[part][...], w_msg[...])
            value = (preact * sigmoid(preact)).astype(BF)
            for block in range(z.blocks):
                msg[part * z.blocks + block] = value[block * z.rows : (block + 1) * z.rows, :]

        for copy in copies[3:]:
            copy.wait()
        acc[...] = jnp.zeros_like(acc)

        def gather_tile(t, carry):
            r = recv[t]
            acc[r] = acc[r] + mm(kern[t], msg[z.place_of(send[t])])
            return carry

        lax.fori_loop(0, z.tiles, gather_tile, 0, unroll=8)
        aggregate = acc[...].reshape(z.nodes, z.width).astype(BF)
        agg[...] = aggregate
        own = latent[...]
        mixed = mm(jnp.concatenate([own, aggregate], axis=1), w_node[...])
        sig = sigmoid(mixed)
        factor[...] = sig * (1.0 + mixed * (1.0 - sig))
        new_rows = (own.astype(F32) + mixed * sig).astype(BF)
        outgoing[...] = mm(place[...], new_rows).astype(BF)

        w_msg_t = jnp.transpose(w_msg[...].astype(F32)).astype(BF)
        for part in range(z.spaces):
            pre_slope[part] = slope_of(mm_nt(w_msg_t, lats[part][...]))

    return pl.pallas_call(
        kernel,
        out_shape=(
            jax.ShapeDtypeStruct((z.slots, z.width), BF),
            jax.ShapeDtypeStruct((1, z.nodes), F32),
            jax.ShapeDtypeStruct((z.nodes, z.width), F32),
            jax.ShapeDtypeStruct((z.nodes, z.width), BF),
            jax.ShapeDtypeStruct((z.spaces, z.width, z.nodes), F32),
        ),
        in_specs=[ANY] * 7 + [VMEM] * (z.spaces - 1),
        out_specs=[VMEM] * 5,
        scratch_shapes=[
            pltpu.SMEM((z.tiles,), jnp.int32),
            pltpu.SMEM((z.tiles,), jnp.int32),
            pltpu.VMEM((1, z.nodes), jnp.int32),
            pltpu.VMEM((z.width, z.width), BF),
            pltpu.VMEM((2 * z.width, z.width), BF),
            pltpu.VMEM((z.tiles, z.rows, z.rows), BF),
            pltpu.VMEM((z.spaces * z.blocks, z.rows, z.width), BF),
            pltpu.VMEM((z.blocks, z.rows, z.width), F32),
            pltpu.VMEM((z.slots, z.nodes), BF),
            pltpu.VMEM((z.nodes, z.width), BF),
            pltpu.SemaphoreType.DMA((7,)),
        ],
        cost_estimate=pl.CostEstimate(
            flops=10_000_000_000, bytes_accessed=1000, transcendentals=0
        ),
        compiler_params=pltpu.CompilerParams(vmem_limit_bytes=24 << 20),
        name="forward",
    )


def backward_call(z):
    lanes = 2 * z.half * z.nodes
    low = z.width // 2

    def kernel(recv_hbm, send_hbm, kern_hbm, w_msg_hbm, w_node_hbm, lat_hbm, returned, slot,
               factor, agg, pre_slope, *rest):
        others, rest = rest[: z.spaces - 1], rest[z.spaces - 1 :]
        payload, keep, grad_keep, direct = rest[:4]
        recv, send, w_msg, w_node, kern, place_t, back, spread, latent, sems = rest[4:]
        lats = (latent, *others)
        copies = [
            pltpu.make_async_copy(src, dst, sems.at[i])
            for i, (src, dst) in enumerate(
                [
                    (w_node_hbm, w_node),
                    (recv_hbm, recv),
                    (send_hbm, send),
                    (kern_hbm, kern),
                    (w_msg_hbm, w_msg),
                    (lat_hbm, latent),
                ]
            )
        ]
        for copy in copies:
            copy.start()
        slot_col = jnp.transpose(jnp.broadcast_to(slot[...], (128, z.nodes))).astype(jnp.int32)
        for at in range(0, z.slots, 128):
            across = iota((z.nodes, 128), 1) + at
            place_t[:, at : at + 128] = (across == slot_col).astype(F32).astype(BF)
        incoming = mm(place_t[...], returned[...])
        slope = incoming * factor[...]
        slope_t = jnp.transpose(slope).astype(BF)
        slope = slope.astype(BF)
        copies[0].wait()
        back_t = mm(w_node[z.width : 2 * z.width, :], slope_t).astype(BF)
        for block in range(z.blocks):
            back[block] = back_t[:, block * z.rows : (block + 1) * z.rows]
        spread[...] = jnp.zeros_like(spread)
        for copy in copies[1:]:
            copy.wait()

        def spread_tile(t, carry):
            s = z.place_of(send[t])
            spread[s] = spread[s] + mm(back[recv[t]], kern[t])
            return carry

        lax.fori_loop(0, z.tiles, spread_tile, 0, unroll=8)

        joined = jnp.concatenate([lats[0][...], agg[...]], axis=1)
        grad_node = mm(slope_t, joined)
        direct[...] = (mm_nt(slope, w_node[0 : z.width, :]) + incoming).astype(BF)
        grad_msg = jnp.zeros((z.width, z.width), F32)
        for step in range(z.half):
            for other in range(2):
                part = 2 * ((-step) % z.half) + other
                total = jnp.concatenate(
                    [spread[part * z.blocks + block] for block in range(z.blocks)], axis=1
                )
                preact_grad = (total * pre_slope[part]).astype(BF)
                grad_msg += mm(preact_grad, lats[part][...])
                back_lat = mm(w_msg[...], preact_grad)
                if other:
                    at = step * z.nodes
                    payload[:, at : at + z.nodes] = back_lat[:low].astype(BF)
                    at += z.half * z.nodes
                    payload[:, at : at + z.nodes] = back_lat[low:].astype(BF)
                else:
                    keep[step] = back_lat
        grads = jnp.concatenate([grad_msg, grad_node], axis=1)
        first = (lax.axis_index("space") & 1) == 0
        grad_keep[...] = jnp.where(first, grads[:low], grads[low:])
        payload[:, lanes:] = jnp.where(first, grads[low:], grads[:low]).astype(BF)

    return pl.pallas_call(
        kernel,
        out_shape=(
            jax.ShapeDtypeStruct((low, lanes + 3 * z.width), BF),
            jax.ShapeDtypeStruct((z.half, z.width, z.nodes), F32),
            jax.ShapeDtypeStruct((low, 3 * z.width), F32),
            jax.ShapeDtypeStruct((z.nodes, z.width), BF),
        ),
        in_specs=[ANY] * 6 + [VMEM] * (4 + z.spaces),
        out_specs=[VMEM] * 4,
        scratch_shapes=[
            pltpu.SMEM((z.tiles,), jnp.int32),
            pltpu.SMEM((z.tiles,), jnp.int32),
            pltpu.VMEM((z.width, z.width), BF),
            pltpu.VMEM((2 * z.width, z.width), BF),
            pltpu.VMEM((z.tiles, z.rows, z.rows), BF),
            pltpu.VMEM((z.nodes, z.slots), BF),
            pltpu.VMEM((z.blocks, z.width, z.rows), BF),
            pltpu.VMEM((z.spaces * z.blocks, z.width, z.rows), F32),
            pltpu.VMEM((z.nodes, z.width), BF),
            pltpu.SemaphoreType.DMA((6,)),
        ],
        cost_estimate=pl.CostEstimate(
            flops=1000000, bytes_accessed=1000, transcendentals=0
        ),
        compiler_params=pltpu.CompilerParams(vmem_limit_bytes=24 << 20),
        name="backward",
    )


def pair_call(z):
    lanes = 2 * z.half * z.nodes
    low = z.width // 2

    def kernel(payload, keep, grad_keep, *outs):
        grad, own, sent = outs[0], outs[1], outs[2:]
        grad[...] = (grad_keep[...] + payload[:, lanes:].astype(F32)).astype(BF)
        for step in range(z.half):
            at = step * z.nodes
            top = payload[:, at : at + z.nodes].astype(F32)
            at += z.half * z.nodes
            bottom = payload[:, at : at + z.nodes].astype(F32)
            total = keep[step] + jnp.concatenate([top, bottom], axis=0)
            if step:
                sent[step - 1][...] = total.astype(BF)
            else:
                own[...] = total

    return pl.pallas_call(
        kernel,
        out_shape=(
            jax.ShapeDtypeStruct((low, 3 * z.width), BF),
            jax.ShapeDtypeStruct((z.width, z.nodes), F32),
            *[jax.ShapeDtypeStruct((z.width, z.nodes), BF)] * (z.half - 1),
        ),
        in_specs=[VMEM] * 3,
        out_specs=[VMEM] * (1 + z.half),
        compiler_params=pltpu.CompilerParams(vmem_limit_bytes=8 << 20),
        name="pair",
    )


def finish_call(z):
    def kernel(direct, own, *rest):
        total = own[...]
        for ref in rest[:-1]:
            total = total + ref[...].astype(F32)
        rest[-1][...] = (jnp.transpose(total) + direct[...].astype(F32)).astype(BF)

    return pl.pallas_call(
        kernel,
        out_shape=jax.ShapeDtypeStruct((z.nodes, z.width), BF),
        in_specs=[VMEM] * (1 + z.half),
        compiler_params=pltpu.CompilerParams(vmem_limit_bytes=8 << 20),
        name="finish",
    )


def weights_call(z):
    def kernel(mine, other, updated, grad_msg, grad_node, updated_out, sem):
        copy = pltpu.make_async_copy(updated, updated_out, sem)
        copy.start()
        first = (lax.axis_index("space") & 1) == 0
        mine, other = mine[...], other[...]
        total = jnp.concatenate(
            [jnp.where(first, mine, other), jnp.where(first, other, mine)], axis=0
        )
        grad_msg[...] = jnp.transpose(total[:, : z.width])
        grad_node[...] = jnp.transpose(total[:, z.width :])
        copy.wait()

    return pl.pallas_call(
        kernel,
        out_shape=(
            jax.ShapeDtypeStruct((z.width, z.width), F32),
            jax.ShapeDtypeStruct((2 * z.width, z.width), F32),
            jax.ShapeDtypeStruct((z.slots, z.width), BF),
        ),
        in_specs=[VMEM] * 3,
        out_specs=[pl.BlockSpec(), pl.BlockSpec(), ANY],
        scratch_shapes=[pltpu.SemaphoreType.DMA],
        compiler_params=pltpu.CompilerParams(vmem_limit_bytes=8 << 20),
        name="weights",
    )


def body(latent, owner_ids, tile_recv, tile_send, kernels, w_msg, w_node, upstream):
    z = Sizes(latent, kernels, upstream)
    devices = z.groups * z.spaces

    def swap(value):
        return lax.all_to_all(
            value.reshape(z.groups, z.capacity, z.width),
            "group", split_axis=0, concat_axis=0, tiled=True,
        ).reshape(z.slots, z.width)

    def to_core(value):
        return lax.ppermute(value, "space", [(i, i ^ 1) for i in range(z.spaces)])

    def along(value, step):
        return lax.ppermute(
            value, "space", [(i, (i + 2 * step) % z.spaces) for i in range(z.spaces)]
        )

    def flip(value, mask):
        return lax.ppermute(value, ("group", "space"), [(i, i ^ mask) for i in range(devices)])

    lats = [
        lax.ppermute(
            latent, "space", [(i, (i + 2 * step) % z.spaces ^ other) for i in range(z.spaces)]
        )
        for step in range(z.half)
        for other in range(2)
        if step or other
    ]
    returned = swap(upstream)
    params = [in_hbm(one) for one in (tile_recv, tile_send, kernels, w_msg, w_node, latent)]
    owners = in_hbm(owner_ids.reshape(1, z.nodes))
    outgoing, slot, factor, agg, pre_slope = forward_call(z)(
        params[0], params[1], owners, *params[2:], *lats
    )
    updated = swap(outgoing)
    payload, keep, grad_keep, direct = backward_call(z)(
        *params, returned, slot, factor, agg, pre_slope, *lats
    )
    grad, own, *sent = pair_call(z)(to_core(payload), keep, grad_keep)

    bits = devices.bit_length() - 1
    for at in range(1, bits, 2):
        span = min(2, bits - at)
        grad = grad.astype(BF)
        got = [grad] + [flip(grad, step << at) for step in range(1, 1 << span)]
        got = [one.astype(F32) for one in got]
        grad = got[0] + got[1]
        if span == 2:
            grad = grad + (got[2] + got[3])
    got = [along(part, step + 1) for step, part in enumerate(sent)]
    latent_grad = finish_call(z)(direct, own, *got)
    grad, updated = lax.optimization_barrier((grad, updated))
    grad_msg, grad_node, updated = weights_call(z)(grad, to_core(grad), updated)
    return updated, latent_grad, grad_msg, grad_node


def solution(mesh):
    split = P(("group", "space"))
    wide = P(("group", "space"), None)
    return jax.shard_map(
        body,
        mesh=mesh,
        in_specs=(wide, wide, split, split, P(("group", "space"), None, None), P(), P(), wide),
        out_specs=(wide, wide, P(), P()),
        check_vma=False,
    )
```

```python
import jax
import jax.numpy as jnp
from jax import lax
from jax.experimental import pallas as pl
from jax.experimental.pallas import tpu as pltpu
from jax.sharding import PartitionSpec as P

BF = jnp.bfloat16
CHUNKS = 4
F32 = jnp.float32
VMEM = pl.BlockSpec(memory_space=pltpu.VMEM)
ANY = pl.BlockSpec(memory_space=pltpu.HBM)


def mm(left, right):
    return jnp.dot(left, right, preferred_element_type=F32)


def mm_nt(left, right):
    return lax.dot_general(left, right, (((1,), (1,)), ((), ())), preferred_element_type=F32)


def sigmoid(value):
    return 0.5 * jnp.tanh(0.5 * value) + 0.5


def slope_of(value):
    sig = sigmoid(value)
    return sig * (1.0 + value * (1.0 - sig))


def in_hbm(value):
    return pltpu.with_memory_space_constraint(value, pltpu.HBM)


def iota(shape, axis):
    return lax.broadcasted_iota(jnp.int32, shape, axis)


class Sizes:
    def __init__(self, latent, kernels, upstream):
        self.nodes, self.width = latent.shape
        self.tiles, self.rows, _ = kernels.shape
        self.groups, self.spaces = lax.axis_size("group"), lax.axis_size("space")
        self.slots = upstream.shape[0]
        self.capacity = self.slots // self.groups
        self.blocks = self.nodes // self.rows
        self.half = self.spaces // 2
        self.chunk = self.tiles // CHUNKS
        self.hot = max(16, -(-self.groups // 16) * 16)

    def tile_copies(self, kern_hbm, kern, sems, first):
        return [
            pltpu.make_async_copy(
                kern_hbm.at[pl.ds(i * self.chunk, self.chunk)],
                kern.at[pl.ds(i * self.chunk, self.chunk)],
                sems.at[first + i],
            )
            for i in range(CHUNKS)
        ]

    def each_tile(self, step, copies):
        for i, copy in enumerate(copies):
            copy.wait()
            for t in range(i * self.chunk, (i + 1) * self.chunk):
                step(t)

    def place_of(self, sender):
        me = lax.axis_index("space")
        device = sender // self.blocks
        step = lax.rem((me >> 1) - (device >> 1) + self.half, self.half)
        other = (me & 1) ^ (device & 1)
        return (2 * step + other) * self.blocks + lax.rem(sender, self.blocks)


def forward_call(z):
    def kernel(recv_hbm, send_hbm, owner_hbm, kern_hbm, w_msg_hbm, w_node_hbm, lat_hbm, *rest):
        others, rest = rest[: z.spaces - 1], rest[z.spaces - 1 :]
        outgoing, slot_out, factor, agg, pre_slope = rest[:5]
        recv, send, owner, w_msg, w_node, kern, msg, acc, place, latent, sems = rest[5:]
        lats = (latent, *others)
        copies = [
            pltpu.make_async_copy(src, dst, sems.at[i])
            for i, (src, dst) in enumerate(
                [
                    (owner_hbm, owner),
                    (w_msg_hbm, w_msg),
                    (lat_hbm, latent),
                    (recv_hbm, recv),
                    (send_hbm, send),
                    (w_node_hbm, w_node),
                ]
            )
        ]
        copies += z.tile_copies(kern_hbm, kern, sems, len(copies))
        for copy in copies:
            copy.start()
        copies[0].wait()

        owner_row = owner[...]
        hot = (iota((z.hot, z.nodes), 0) == owner_row).astype(F32)
        before = (iota((z.nodes, z.nodes), 0) < iota((z.nodes, z.nodes), 1)).astype(F32)
        counts = mm(hot.astype(BF), before.astype(BF))
        rank = jnp.sum(counts * hot, axis=0, keepdims=True)
        slot = owner_row.astype(F32) * z.capacity + rank
        slot_row = slot.astype(jnp.int32)
        slot_out[...] = slot
        for at in range(0, z.slots, 128):
            down = iota((128, z.nodes), 0) + at
            place[at : at + 128, :] = (down == slot_row).astype(F32).astype(BF)

        copies[1].wait()
        copies[2].wait()
        for part in range(z.spaces):
            preact = mm(lats[part][...], w_msg[...])
            value = (preact * sigmoid(preact)).astype(BF)
            for block in range(z.blocks):
                msg[part * z.blocks + block] = value[block * z.rows : (block + 1) * z.rows, :]

        for copy in copies[3:6]:
            copy.wait()
        acc[...] = jnp.zeros_like(acc)

        def gather_tile(t):
            r = recv[t]
            acc[r] = acc[r] + mm(kern[t], msg[z.place_of(send[t])])

        z.each_tile(gather_tile, copies[6:])
        aggregate = acc[...].reshape(z.nodes, z.width).astype(BF)
        agg[...] = aggregate
        own = latent[...]
        mixed = mm(jnp.concatenate([own, aggregate], axis=1), w_node[...])
        sig = sigmoid(mixed)
        factor[...] = sig * (1.0 + mixed * (1.0 - sig))
        new_rows = (own.astype(F32) + mixed * sig).astype(BF)
        outgoing[...] = mm(place[...], new_rows).astype(BF)

        w_msg_t = jnp.transpose(w_msg[...].astype(F32)).astype(BF)
        for part in range(z.spaces):
            pre_slope[part] = slope_of(mm_nt(w_msg_t, lats[part][...]))

    return pl.pallas_call(
        kernel,
        out_shape=(
            jax.ShapeDtypeStruct((z.slots, z.width), BF),
            jax.ShapeDtypeStruct((1, z.nodes), F32),
            jax.ShapeDtypeStruct((z.nodes, z.width), F32),
            jax.ShapeDtypeStruct((z.nodes, z.width), BF),
            jax.ShapeDtypeStruct((z.spaces, z.width, z.nodes), F32),
        ),
        in_specs=[ANY] * 7 + [VMEM] * (z.spaces - 1),
        out_specs=[VMEM] * 5,
        scratch_shapes=[
            pltpu.SMEM((z.tiles,), jnp.int32),
            pltpu.SMEM((z.tiles,), jnp.int32),
            pltpu.VMEM((1, z.nodes), jnp.int32),
            pltpu.VMEM((z.width, z.width), BF),
            pltpu.VMEM((2 * z.width, z.width), BF),
            pltpu.VMEM((z.tiles, z.rows, z.rows), BF),
            pltpu.VMEM((z.spaces * z.blocks, z.rows, z.width), BF),
            pltpu.VMEM((z.blocks, z.rows, z.width), F32),
            pltpu.VMEM((z.slots, z.nodes), BF),
            pltpu.VMEM((z.nodes, z.width), BF),
            pltpu.SemaphoreType.DMA((6 + CHUNKS,)),
        ],
        cost_estimate=pl.CostEstimate(
            flops=10_000_000_000, bytes_accessed=1000, transcendentals=0
        ),
        compiler_params=pltpu.CompilerParams(vmem_limit_bytes=24 << 20),
        name="forward",
    )


def backward_call(z):
    lanes = 2 * z.half * z.nodes
    low = z.width // 2

    def kernel(recv_hbm, send_hbm, kern_hbm, w_msg_hbm, w_node_hbm, lat_hbm, returned, slot,
               factor, agg, pre_slope, *rest):
        others, rest = rest[: z.spaces - 1], rest[z.spaces - 1 :]
        payload, keep, grad_keep, direct = rest[:4]
        recv, send, w_msg, w_node, kern, place_t, back, spread, latent, sems = rest[4:]
        lats = (latent, *others)
        copies = [
            pltpu.make_async_copy(src, dst, sems.at[i])
            for i, (src, dst) in enumerate(
                [
                    (w_node_hbm, w_node),
                    (recv_hbm, recv),
                    (send_hbm, send),
                    (w_msg_hbm, w_msg),
                    (lat_hbm, latent),
                ]
            )
        ]
        copies += z.tile_copies(kern_hbm, kern, sems, len(copies))
        for copy in copies:
            copy.start()
        slot_col = jnp.transpose(jnp.broadcast_to(slot[...], (128, z.nodes))).astype(jnp.int32)
        for at in range(0, z.slots, 128):
            across = iota((z.nodes, 128), 1) + at
            place_t[:, at : at + 128] = (across == slot_col).astype(F32).astype(BF)
        incoming = mm(place_t[...], returned[...])
        slope = incoming * factor[...]
        slope_t = jnp.transpose(slope).astype(BF)
        slope = slope.astype(BF)
        copies[0].wait()
        back_t = mm(w_node[z.width : 2 * z.width, :], slope_t).astype(BF)
        for block in range(z.blocks):
            back[block] = back_t[:, block * z.rows : (block + 1) * z.rows]
        spread[...] = jnp.zeros_like(spread)
        copies[1].wait()
        copies[2].wait()

        def spread_tile(t):
            s = z.place_of(send[t])
            spread[s] = spread[s] + mm(back[recv[t]], kern[t])

        z.each_tile(spread_tile, copies[5:])
        copies[3].wait()
        copies[4].wait()

        joined = jnp.concatenate([lats[0][...], agg[...]], axis=1)
        grad_node = mm(slope_t, joined)
        direct[...] = (mm_nt(slope, w_node[0 : z.width, :]) + incoming).astype(BF)
        grad_msg = jnp.zeros((z.width, z.width), F32)
        for step in range(z.half):
            for other in range(2):
                part = 2 * ((-step) % z.half) + other
                total = jnp.concatenate(
                    [spread[part * z.blocks + block] for block in range(z.blocks)], axis=1
                )
                preact_grad = (total * pre_slope[part]).astype(BF)
                grad_msg += mm(preact_grad, lats[part][...])
                back_lat = mm(w_msg[...], preact_grad)
                if other:
                    at = step * z.nodes
                    payload[:, at : at + z.nodes] = back_lat[:low].astype(BF)
                    at += z.half * z.nodes
                    payload[:, at : at + z.nodes] = back_lat[low:].astype(BF)
                else:
                    keep[step] = back_lat
        grads = jnp.concatenate([grad_msg, grad_node], axis=1)
        first = (lax.axis_index("space") & 1) == 0
        grad_keep[...] = jnp.where(first, grads[:low], grads[low:])
        payload[:, lanes:] = jnp.where(first, grads[low:], grads[:low]).astype(BF)

    return pl.pallas_call(
        kernel,
        out_shape=(
            jax.ShapeDtypeStruct((low, lanes + 3 * z.width), BF),
            jax.ShapeDtypeStruct((z.half, z.width, z.nodes), F32),
            jax.ShapeDtypeStruct((low, 3 * z.width), F32),
            jax.ShapeDtypeStruct((z.nodes, z.width), BF),
        ),
        in_specs=[ANY] * 6 + [VMEM] * (4 + z.spaces),
        out_specs=[VMEM] * 4,
        scratch_shapes=[
            pltpu.SMEM((z.tiles,), jnp.int32),
            pltpu.SMEM((z.tiles,), jnp.int32),
            pltpu.VMEM((z.width, z.width), BF),
            pltpu.VMEM((2 * z.width, z.width), BF),
            pltpu.VMEM((z.tiles, z.rows, z.rows), BF),
            pltpu.VMEM((z.nodes, z.slots), BF),
            pltpu.VMEM((z.blocks, z.width, z.rows), BF),
            pltpu.VMEM((z.spaces * z.blocks, z.width, z.rows), F32),
            pltpu.VMEM((z.nodes, z.width), BF),
            pltpu.SemaphoreType.DMA((5 + CHUNKS,)),
        ],
        cost_estimate=pl.CostEstimate(
            flops=1000000, bytes_accessed=1000, transcendentals=0
        ),
        compiler_params=pltpu.CompilerParams(vmem_limit_bytes=24 << 20),
        name="backward",
    )


def pair_call(z):
    lanes = 2 * z.half * z.nodes
    low = z.width // 2

    def kernel(payload, keep, grad_keep, *outs):
        grad, own, sent = outs[0], outs[1], outs[2:]
        grad[...] = (grad_keep[...] + payload[:, lanes:].astype(F32)).astype(BF)
        for step in range(z.half):
            at = step * z.nodes
            top = payload[:, at : at + z.nodes].astype(F32)
            at += z.half * z.nodes
            bottom = payload[:, at : at + z.nodes].astype(F32)
            total = keep[step] + jnp.concatenate([top, bottom], axis=0)
            if step:
                sent[step - 1][...] = total.astype(BF)
            else:
                own[...] = total

    return pl.pallas_call(
        kernel,
        out_shape=(
            jax.ShapeDtypeStruct((low, 3 * z.width), BF),
            jax.ShapeDtypeStruct((z.width, z.nodes), F32),
            *[jax.ShapeDtypeStruct((z.width, z.nodes), BF)] * (z.half - 1),
        ),
        in_specs=[VMEM] * 3,
        out_specs=[VMEM] * (1 + z.half),
        compiler_params=pltpu.CompilerParams(vmem_limit_bytes=8 << 20),
        name="pair",
    )


def finish_call(z):
    def kernel(direct, own, *rest):
        total = own[...]
        for ref in rest[:-1]:
            total = total + ref[...].astype(F32)
        rest[-1][...] = (jnp.transpose(total) + direct[...].astype(F32)).astype(BF)

    return pl.pallas_call(
        kernel,
        out_shape=jax.ShapeDtypeStruct((z.nodes, z.width), BF),
        in_specs=[VMEM] * (1 + z.half),
        compiler_params=pltpu.CompilerParams(vmem_limit_bytes=8 << 20),
        name="finish",
    )


def weights_call(z):
    def kernel(mine, other, grad_msg, grad_node):
        first = (lax.axis_index("space") & 1) == 0
        mine, other = mine[...], other[...]
        total = jnp.concatenate(
            [jnp.where(first, mine, other), jnp.where(first, other, mine)], axis=0
        )
        grad_msg[...] = jnp.transpose(total[:, : z.width])
        grad_node[...] = jnp.transpose(total[:, z.width :])

    return pl.pallas_call(
        kernel,
        out_shape=(
            jax.ShapeDtypeStruct((z.width, z.width), F32),
            jax.ShapeDtypeStruct((2 * z.width, z.width), F32),
        ),
        in_specs=[VMEM] * 2,
        compiler_params=pltpu.CompilerParams(vmem_limit_bytes=8 << 20),
        name="weights",
    )


def emit_call(z):
    def kernel(rows, out, sem):
        copy = pltpu.make_async_copy(rows, out, sem)
        copy.start()
        copy.wait()

    return pl.pallas_call(
        kernel,
        out_shape=jax.ShapeDtypeStruct((z.slots, z.width), BF),
        in_specs=[VMEM],
        out_specs=ANY,
        scratch_shapes=[pltpu.SemaphoreType.DMA],
        compiler_params=pltpu.CompilerParams(vmem_limit_bytes=8 << 20),
        name="emit",
    )


def body(latent, owner_ids, tile_recv, tile_send, kernels, w_msg, w_node, upstream):
    z = Sizes(latent, kernels, upstream)
    devices = z.groups * z.spaces

    def swap(value):
        return lax.all_to_all(
            value.reshape(z.groups, z.capacity, z.width),
            "group", split_axis=0, concat_axis=0, tiled=True,
        ).reshape(z.slots, z.width)

    def to_core(value):
        return lax.ppermute(value, "space", [(i, i ^ 1) for i in range(z.spaces)])

    def along(value, step):
        return lax.ppermute(
            value, "space", [(i, (i + 2 * step) % z.spaces) for i in range(z.spaces)]
        )

    def flip(value, mask):
        return lax.ppermute(value, ("group", "space"), [(i, i ^ mask) for i in range(devices)])

    lats = [
        lax.ppermute(
            latent, "space", [(i, (i + 2 * step) % z.spaces ^ other) for i in range(z.spaces)]
        )
        for step in range(z.half)
        for other in range(2)
        if step or other
    ]
    returned = swap(upstream)
    params = [in_hbm(one) for one in (tile_recv, tile_send, kernels, w_msg, w_node, latent)]
    owners = in_hbm(owner_ids.reshape(1, z.nodes))
    outgoing, slot, factor, agg, pre_slope = forward_call(z)(
        params[0], params[1], owners, *params[2:], *lats
    )
    updated = swap(outgoing)
    payload, keep, grad_keep, direct = backward_call(z)(
        *params, returned, slot, factor, agg, pre_slope, *lats
    )
    grad, own, *sent = pair_call(z)(to_core(payload), keep, grad_keep)

    got = [along(part, step + 1) for step, part in enumerate(sent)]
    latent_grad = finish_call(z)(direct, own, *got)

    bits = devices.bit_length() - 1
    for at in range(1, bits, 2):
        span = min(2, bits - at)
        grad = grad.astype(BF)
        got = [grad] + [flip(grad, step << at) for step in range(1, 1 << span)]
        if at + 2 >= bits:
            got[-1], latent_grad = lax.optimization_barrier((got[-1], latent_grad))
        got = [one.astype(F32) for one in got]
        grad = got[0] + got[1]
        if span == 2:
            grad = grad + (got[2] + got[3])
    grad, updated = lax.optimization_barrier((grad, updated))
    updated = emit_call(z)(updated)
    grad_msg, grad_node = weights_call(z)(grad, to_core(grad))
    return updated, latent_grad, grad_msg, grad_node


def solution(mesh):
    split = P(("group", "space"))
    wide = P(("group", "space"), None)
    return jax.shard_map(
        body,
        mesh=mesh,
        in_specs=(wide, wide, split, split, P(("group", "space"), None, None), P(), P(), wide),
        out_specs=(wide, wide, P(), P()),
        check_vma=False,
    )
```

```python
import jax
import jax.numpy as jnp
from jax import lax
from jax.experimental import pallas as pl
from jax.experimental.pallas import tpu as pltpu
from jax.sharding import PartitionSpec as P

BF = jnp.bfloat16
CHUNKS = 2
F32 = jnp.float32
VMEM = pl.BlockSpec(memory_space=pltpu.VMEM)
ANY = pl.BlockSpec(memory_space=pltpu.HBM)


def mm(left, right):
    return jnp.dot(left, right, preferred_element_type=F32)


def mm_nt(left, right):
    return lax.dot_general(left, right, (((1,), (1,)), ((), ())), preferred_element_type=F32)


def sigmoid(value):
    return 0.5 * jnp.tanh(0.5 * value) + 0.5


def slope_of(value):
    sig = sigmoid(value)
    return sig * (1.0 + value * (1.0 - sig))


def in_hbm(value):
    return pltpu.with_memory_space_constraint(value, pltpu.HBM)


def iota(shape, axis):
    return lax.broadcasted_iota(jnp.int32, shape, axis)


class Sizes:
    def __init__(self, latent, kernels, upstream):
        self.nodes, self.width = latent.shape
        self.tiles, self.rows, _ = kernels.shape
        self.groups, self.spaces = lax.axis_size("group"), lax.axis_size("space")
        self.slots = upstream.shape[0]
        self.capacity = self.slots // self.groups
        self.blocks = self.nodes // self.rows
        self.half = self.spaces // 2
        self.chunk = self.tiles // CHUNKS
        self.hot = max(16, -(-self.groups // 16) * 16)

    def tile_copies(self, kern_hbm, kern, sems, first):
        return [
            pltpu.make_async_copy(
                kern_hbm.at[pl.ds(i * self.chunk, self.chunk)],
                kern.at[pl.ds(i * self.chunk, self.chunk)],
                sems.at[first + i],
            )
            for i in range(CHUNKS)
        ]

    def each_tile(self, step, copies):
        for i, copy in enumerate(copies):
            copy.wait()
            for t in range(i * self.chunk, (i + 1) * self.chunk):
                step(t)

    def place_of(self, sender):
        me = lax.axis_index("space")
        device = sender // self.blocks
        step = lax.rem((me >> 1) - (device >> 1) + self.half, self.half)
        other = (me & 1) ^ (device & 1)
        return (2 * step + other) * self.blocks + lax.rem(sender, self.blocks)


def forward_call(z):
    def kernel(recv_hbm, send_hbm, owner_hbm, kern_hbm, w_msg_hbm, w_node_hbm, lat_hbm, *rest):
        others, rest = rest[: z.spaces - 1], rest[z.spaces - 1 :]
        outgoing, slot_out, factor, agg, pre_slope = rest[:5]
        recv, send, owner, w_msg, w_node, kern, msg, acc, place, latent, sems = rest[5:]
        lats = (latent, *others)
        copies = [
            pltpu.make_async_copy(src, dst, sems.at[i])
            for i, (src, dst) in enumerate(
                [
                    (owner_hbm, owner),
                    (w_msg_hbm, w_msg),
                    (lat_hbm, latent),
                    (recv_hbm, recv),
                    (send_hbm, send),
                    (w_node_hbm, w_node),
                ]
            )
        ]
        copies += z.tile_copies(kern_hbm, kern, sems, len(copies))
        for copy in copies:
            copy.start()
        copies[0].wait()

        owner_row = owner[...]
        hot = (iota((z.hot, z.nodes), 0) == owner_row).astype(F32)
        before = (iota((z.nodes, z.nodes), 0) < iota((z.nodes, z.nodes), 1)).astype(F32)
        counts = mm(hot.astype(BF), before.astype(BF))
        rank = jnp.sum(counts * hot, axis=0, keepdims=True)
        slot = owner_row.astype(F32) * z.capacity + rank
        slot_row = slot.astype(jnp.int32)
        slot_out[...] = slot
        for at in range(0, z.slots, 128):
            down = iota((128, z.nodes), 0) + at
            place[at : at + 128, :] = (down == slot_row).astype(F32).astype(BF)

        copies[1].wait()
        copies[2].wait()
        for part in range(z.spaces):
            preact = mm(lats[part][...], w_msg[...])
            value = (preact * sigmoid(preact)).astype(BF)
            for block in range(z.blocks):
                msg[part * z.blocks + block] = value[block * z.rows : (block + 1) * z.rows, :]

        for copy in copies[3:6]:
            copy.wait()
        acc[...] = jnp.zeros_like(acc)

        def gather_tile(t):
            r = recv[t]
            acc[r] = acc[r] + mm(kern[t], msg[z.place_of(send[t])])

        z.each_tile(gather_tile, copies[6:])
        aggregate = acc[...].reshape(z.nodes, z.width).astype(BF)
        agg[...] = aggregate
        own = latent[...]
        mixed = mm(jnp.concatenate([own, aggregate], axis=1), w_node[...])
        sig = sigmoid(mixed)
        factor[...] = jnp.transpose(sig * (1.0 + mixed * (1.0 - sig)))
        new_rows = (own.astype(F32) + mixed * sig).astype(BF)
        outgoing[...] = mm(place[...], new_rows).astype(BF)

        w_msg_t = jnp.transpose(w_msg[...].astype(F32)).astype(BF)
        for part in range(z.spaces):
            pre_slope[part] = slope_of(mm_nt(w_msg_t, lats[part][...]))

    return pl.pallas_call(
        kernel,
        out_shape=(
            jax.ShapeDtypeStruct((z.slots, z.width), BF),
            jax.ShapeDtypeStruct((1, z.nodes), F32),
            jax.ShapeDtypeStruct((z.width, z.nodes), F32),
            jax.ShapeDtypeStruct((z.nodes, z.width), BF),
            jax.ShapeDtypeStruct((z.spaces, z.width, z.nodes), F32),
        ),
        in_specs=[ANY] * 7 + [VMEM] * (z.spaces - 1),
        out_specs=[VMEM] * 5,
        scratch_shapes=[
            pltpu.SMEM((z.tiles,), jnp.int32),
            pltpu.SMEM((z.tiles,), jnp.int32),
            pltpu.VMEM((1, z.nodes), jnp.int32),
            pltpu.VMEM((z.width, z.width), BF),
            pltpu.VMEM((2 * z.width, z.width), BF),
            pltpu.VMEM((z.tiles, z.rows, z.rows), BF),
            pltpu.VMEM((z.spaces * z.blocks, z.rows, z.width), BF),
            pltpu.VMEM((z.blocks, z.rows, z.width), F32),
            pltpu.VMEM((z.slots, z.nodes), BF),
            pltpu.VMEM((z.nodes, z.width), BF),
            pltpu.SemaphoreType.DMA((6 + CHUNKS,)),
        ],
        cost_estimate=pl.CostEstimate(
            flops=10_000_000_000, bytes_accessed=1000, transcendentals=0
        ),
        compiler_params=pltpu.CompilerParams(vmem_limit_bytes=24 << 20),
        name="forward",
    )


def backward_call(z):
    lanes = 2 * z.half * z.nodes
    low = z.width // 2

    def kernel(recv_hbm, send_hbm, kern_hbm, w_msg_hbm, w_node_hbm, lat_hbm, returned, slot,
               factor, agg, pre_slope, *rest):
        others, rest = rest[: z.spaces - 1], rest[z.spaces - 1 :]
        payload, keep, grad_keep, direct = rest[:4]
        recv, send, w_msg, w_node, kern, place, back, spread, latent, sems = rest[4:]
        lats = (latent, *others)
        copies = [
            pltpu.make_async_copy(src, dst, sems.at[i])
            for i, (src, dst) in enumerate(
                [
                    (w_node_hbm, w_node),
                    (recv_hbm, recv),
                    (send_hbm, send),
                    (w_msg_hbm, w_msg),
                    (lat_hbm, latent),
                ]
            )
        ]
        copies += z.tile_copies(kern_hbm, kern, sems, len(copies))
        for copy in copies:
            copy.start()
        slot_row = slot[...].astype(jnp.int32)
        for at in range(0, z.slots, 128):
            down = iota((128, z.nodes), 0) + at
            place[at : at + 128, :] = (down == slot_row).astype(F32).astype(BF)
        returned_t = jnp.transpose(returned[...].astype(F32)).astype(BF)
        incoming_t = mm(returned_t, place[...])
        slope_t = (incoming_t * factor[...]).astype(BF)
        copies[0].wait()
        rows_t = mm(w_node[...], slope_t)
        direct[...] = rows_t[: z.width] + incoming_t
        back_t = rows_t[z.width :].astype(BF)
        for block in range(z.blocks):
            back[block] = back_t[:, block * z.rows : (block + 1) * z.rows]
        spread[...] = jnp.zeros_like(spread)
        copies[1].wait()
        copies[2].wait()

        def spread_tile(t):
            s = z.place_of(send[t])
            spread[s] = spread[s] + mm(back[recv[t]], kern[t])

        z.each_tile(spread_tile, copies[5:])
        copies[3].wait()
        copies[4].wait()

        joined = jnp.concatenate([lats[0][...], agg[...]], axis=1)
        grad_node = mm(slope_t, joined)
        grad_msg = jnp.zeros((z.width, z.width), F32)
        for step in range(z.half):
            for other in range(2):
                part = 2 * ((-step) % z.half) + other
                total = jnp.concatenate(
                    [spread[part * z.blocks + block] for block in range(z.blocks)], axis=1
                )
                preact_grad = (total * pre_slope[part]).astype(BF)
                grad_msg += mm(preact_grad, lats[part][...])
                back_lat = mm(w_msg[...], preact_grad)
                if other:
                    at = step * z.nodes
                    payload[:, at : at + z.nodes] = back_lat[:low].astype(BF)
                    at += z.half * z.nodes
                    payload[:, at : at + z.nodes] = back_lat[low:].astype(BF)
                else:
                    keep[step] = back_lat
        grads = jnp.concatenate([grad_msg, grad_node], axis=1)
        first = (lax.axis_index("space") & 1) == 0
        grad_keep[...] = jnp.where(first, grads[:low], grads[low:])
        payload[:, lanes:] = jnp.where(first, grads[low:], grads[:low]).astype(BF)

    return pl.pallas_call(
        kernel,
        out_shape=(
            jax.ShapeDtypeStruct((low, lanes + 3 * z.width), BF),
            jax.ShapeDtypeStruct((z.half, z.width, z.nodes), F32),
            jax.ShapeDtypeStruct((low, 3 * z.width), F32),
            jax.ShapeDtypeStruct((z.width, z.nodes), F32),
        ),
        in_specs=[ANY] * 6 + [VMEM] * (4 + z.spaces),
        out_specs=[VMEM] * 4,
        scratch_shapes=[
            pltpu.SMEM((z.tiles,), jnp.int32),
            pltpu.SMEM((z.tiles,), jnp.int32),
            pltpu.VMEM((z.width, z.width), BF),
            pltpu.VMEM((2 * z.width, z.width), BF),
            pltpu.VMEM((z.tiles, z.rows, z.rows), BF),
            pltpu.VMEM((z.slots, z.nodes), BF),
            pltpu.VMEM((z.blocks, z.width, z.rows), BF),
            pltpu.VMEM((z.spaces * z.blocks, z.width, z.rows), F32),
            pltpu.VMEM((z.nodes, z.width), BF),
            pltpu.SemaphoreType.DMA((5 + CHUNKS,)),
        ],
        cost_estimate=pl.CostEstimate(
            flops=1000000, bytes_accessed=1000, transcendentals=0
        ),
        compiler_params=pltpu.CompilerParams(vmem_limit_bytes=24 << 20),
        name="backward",
    )


def pair_call(z):
    lanes = 2 * z.half * z.nodes
    low = z.width // 2

    def kernel(payload, keep, grad_keep, *outs):
        grad, own, sent = outs[0], outs[1], outs[2:]
        grad[...] = (grad_keep[...] + payload[:, lanes:].astype(F32)).astype(BF)
        for step in range(z.half):
            at = step * z.nodes
            top = payload[:, at : at + z.nodes].astype(F32)
            at += z.half * z.nodes
            bottom = payload[:, at : at + z.nodes].astype(F32)
            total = keep[step] + jnp.concatenate([top, bottom], axis=0)
            if step:
                sent[step - 1][...] = total.astype(BF)
            else:
                own[...] = total

    return pl.pallas_call(
        kernel,
        out_shape=(
            jax.ShapeDtypeStruct((low, 3 * z.width), BF),
            jax.ShapeDtypeStruct((z.width, z.nodes), F32),
            *[jax.ShapeDtypeStruct((z.width, z.nodes), BF)] * (z.half - 1),
        ),
        in_specs=[VMEM] * 3,
        out_specs=[VMEM] * (1 + z.half),
        compiler_params=pltpu.CompilerParams(vmem_limit_bytes=8 << 20),
        name="pair",
    )


def finish_call(z):
    def kernel(direct, own, *rest):
        total = own[...] + direct[...]
        for ref in rest[:-1]:
            total = total + ref[...].astype(F32)
        rest[-1][...] = jnp.transpose(total).astype(BF)

    return pl.pallas_call(
        kernel,
        out_shape=jax.ShapeDtypeStruct((z.nodes, z.width), BF),
        in_specs=[VMEM] * (1 + z.half),
        compiler_params=pltpu.CompilerParams(vmem_limit_bytes=8 << 20),
        name="finish",
    )


def weights_call(z):
    def kernel(mine, other, grad_msg, grad_node):
        first = (lax.axis_index("space") & 1) == 0
        mine, other = mine[...], other[...]
        total = jnp.concatenate(
            [jnp.where(first, mine, other), jnp.where(first, other, mine)], axis=0
        )
        grad_msg[...] = jnp.transpose(total[:, : z.width])
        grad_node[...] = jnp.transpose(total[:, z.width :])

    return pl.pallas_call(
        kernel,
        out_shape=(
            jax.ShapeDtypeStruct((z.width, z.width), F32),
            jax.ShapeDtypeStruct((2 * z.width, z.width), F32),
        ),
        in_specs=[VMEM] * 2,
        compiler_params=pltpu.CompilerParams(vmem_limit_bytes=8 << 20),
        name="weights",
    )


def emit_call(z):
    def kernel(rows, out, sem):
        copy = pltpu.make_async_copy(rows, out, sem)
        copy.start()
        copy.wait()

    return pl.pallas_call(
        kernel,
        out_shape=jax.ShapeDtypeStruct((z.slots, z.width), BF),
        in_specs=[VMEM],
        out_specs=ANY,
        scratch_shapes=[pltpu.SemaphoreType.DMA],
        compiler_params=pltpu.CompilerParams(vmem_limit_bytes=8 << 20),
        name="emit",
    )


def body(latent, owner_ids, tile_recv, tile_send, kernels, w_msg, w_node, upstream):
    z = Sizes(latent, kernels, upstream)
    devices = z.groups * z.spaces

    def swap(value):
        return lax.all_to_all(
            value.reshape(z.groups, z.capacity, z.width),
            "group", split_axis=0, concat_axis=0, tiled=True,
        ).reshape(z.slots, z.width)

    def to_core(value):
        return lax.ppermute(value, "space", [(i, i ^ 1) for i in range(z.spaces)])

    def along(value, step):
        return lax.ppermute(
            value, "space", [(i, (i + 2 * step) % z.spaces) for i in range(z.spaces)]
        )

    def flip(value, mask):
        return lax.ppermute(value, ("group", "space"), [(i, i ^ mask) for i in range(devices)])

    lats = [
        lax.ppermute(
            latent, "space", [(i, (i + 2 * step) % z.spaces ^ other) for i in range(z.spaces)]
        )
        for step in range(z.half)
        for other in range(2)
        if step or other
    ]
    returned = swap(upstream)
    params = [in_hbm(one) for one in (tile_recv, tile_send, kernels, w_msg, w_node, latent)]
    owners = in_hbm(owner_ids.reshape(1, z.nodes))
    outgoing, slot, factor, agg, pre_slope = forward_call(z)(
        params[0], params[1], owners, *params[2:], *lats
    )
    updated = swap(outgoing)
    payload, keep, grad_keep, direct = backward_call(z)(
        *params, returned, slot, factor, agg, pre_slope, *lats
    )
    grad, own, *sent = pair_call(z)(to_core(payload), keep, grad_keep)

    got = [along(part, step + 1) for step, part in enumerate(sent)]
    latent_grad = finish_call(z)(direct, own, *got)

    bits = devices.bit_length() - 1
    for at in reversed(range(1, bits, 2)):
        span = min(2, bits - at)
        grad = grad.astype(BF)
        got = [grad] + [flip(grad, step << at) for step in range(1, 1 << span)]
        if at == 1:
            got[-1], latent_grad = lax.optimization_barrier((got[-1], latent_grad))
        got = [one.astype(F32) for one in got]
        grad = got[0] + got[1]
        if span == 2:
            grad = grad + (got[2] + got[3])
    grad_msg, grad_node = weights_call(z)(grad, to_core(grad))
    grad_msg, updated = lax.optimization_barrier((grad_msg, updated))
    updated = emit_call(z)(updated)
    return updated, latent_grad, grad_msg, grad_node


def solution(mesh):
    split = P(("group", "space"))
    wide = P(("group", "space"), None)
    return jax.shard_map(
        body,
        mesh=mesh,
        in_specs=(wide, wide, split, split, P(("group", "space"), None, None), P(), P(), wide),
        out_specs=(wide, wide, P(), P()),
        check_vma=False,
    )
```

```python
import jax
import jax.numpy as jnp
from jax import lax
from jax.experimental import pallas as pl
from jax.experimental.pallas import tpu as pltpu
from jax.sharding import PartitionSpec as P

BF = jnp.bfloat16
CHUNKS = 2
F32 = jnp.float32
VMEM = pl.BlockSpec(memory_space=pltpu.VMEM)
ANY = pl.BlockSpec(memory_space=pltpu.HBM)


def mm(left, right):
    return jnp.dot(left, right, preferred_element_type=F32)


def mm_nt(left, right):
    return lax.dot_general(left, right, (((1,), (1,)), ((), ())), preferred_element_type=F32)


def sigmoid(value):
    return 0.5 * jnp.tanh(0.5 * value) + 0.5


def slope_of(value):
    sig = sigmoid(value)
    return sig * (1.0 + value * (1.0 - sig))


def in_hbm(value):
    return pltpu.with_memory_space_constraint(value, pltpu.HBM)


def iota(shape, axis):
    return lax.broadcasted_iota(jnp.int32, shape, axis)


class Sizes:
    def __init__(self, latent, kernels, upstream):
        self.nodes, self.width = latent.shape
        self.tiles, self.rows, _ = kernels.shape
        self.groups, self.spaces = lax.axis_size("group"), lax.axis_size("space")
        self.slots = upstream.shape[0]
        self.capacity = self.slots // self.groups
        self.blocks = self.nodes // self.rows
        self.half = self.spaces // 2
        self.chunk = self.tiles // CHUNKS
        self.hot = max(16, -(-self.groups // 16) * 16)

    def tile_copies(self, kern_hbm, kern, sems, first):
        return [
            pltpu.make_async_copy(
                kern_hbm.at[pl.ds(i * self.chunk, self.chunk)],
                kern.at[pl.ds(i * self.chunk, self.chunk)],
                sems.at[first + i],
            )
            for i in range(CHUNKS)
        ]

    def each_tile(self, step, copies):
        for i, copy in enumerate(copies):
            copy.wait()
            for t in range(i * self.chunk, (i + 1) * self.chunk):
                step(t)

    def place_of(self, sender):
        me = lax.axis_index("space")
        device = sender // self.blocks
        step = lax.rem((me >> 1) - (device >> 1) + self.half, self.half)
        other = (me & 1) ^ (device & 1)
        return (2 * step + other) * self.blocks + lax.rem(sender, self.blocks)


def forward_call(z):
    def kernel(recv_hbm, send_hbm, owner_hbm, kern_hbm, w_msg_hbm, w_node_hbm, lat_hbm, *rest):
        others, rest = rest[: z.spaces - 1], rest[z.spaces - 1 :]
        outgoing, slot_out, factor, agg, pre_slope = rest[:5]
        recv, send, owner, w_msg, w_node, kern, msg, acc, place, latent, sems = rest[5:]
        lats = (latent, *others)
        copies = [
            pltpu.make_async_copy(src, dst, sems.at[i])
            for i, (src, dst) in enumerate(
                [
                    (owner_hbm, owner),
                    (w_msg_hbm, w_msg),
                    (lat_hbm, latent),
                    (recv_hbm, recv),
                    (send_hbm, send),
                    (w_node_hbm, w_node),
                ]
            )
        ]
        copies += z.tile_copies(kern_hbm, kern, sems, len(copies))
        for copy in copies:
            copy.start()
        copies[0].wait()

        owner_row = owner[...]
        hot = (iota((z.hot, z.nodes), 0) == owner_row).astype(F32)
        before = (iota((z.nodes, z.nodes), 0) < iota((z.nodes, z.nodes), 1)).astype(F32)
        counts = mm(hot.astype(BF), before.astype(BF))
        rank = jnp.sum(counts * hot, axis=0, keepdims=True)
        slot = owner_row.astype(F32) * z.capacity + rank
        slot_row = slot.astype(jnp.int32)
        slot_out[...] = slot
        for at in range(0, z.slots, 128):
            down = iota((128, z.nodes), 0) + at
            place[at : at + 128, :] = (down == slot_row).astype(F32).astype(BF)

        copies[1].wait()
        copies[2].wait()
        for part in range(z.spaces):
            preact = mm(lats[part][...], w_msg[...])
            value = (preact * sigmoid(preact)).astype(BF)
            for block in range(z.blocks):
                msg[part * z.blocks + block] = value[block * z.rows : (block + 1) * z.rows, :]

        for copy in copies[3:6]:
            copy.wait()
        acc[...] = jnp.zeros_like(acc)

        def gather_tile(t):
            r = recv[t]
            acc[r] = acc[r] + mm(kern[t], msg[z.place_of(send[t])])

        z.each_tile(gather_tile, copies[6:])
        aggregate = acc[...].reshape(z.nodes, z.width).astype(BF)
        agg[...] = aggregate
        own = latent[...]
        mixed = mm(jnp.concatenate([own, aggregate], axis=1), w_node[...])
        sig = sigmoid(mixed)
        factor[...] = jnp.transpose(sig * (1.0 + mixed * (1.0 - sig)))
        new_rows = (own.astype(F32) + mixed * sig).astype(BF)
        outgoing[...] = mm(place[...], new_rows).astype(BF)

        w_msg_t = jnp.transpose(w_msg[...].astype(F32)).astype(BF)
        for part in range(z.spaces):
            pre_slope[part] = slope_of(mm_nt(w_msg_t, lats[part][...]))

    return pl.pallas_call(
        kernel,
        out_shape=(
            jax.ShapeDtypeStruct((z.slots, z.width), BF),
            jax.ShapeDtypeStruct((1, z.nodes), F32),
            jax.ShapeDtypeStruct((z.width, z.nodes), F32),
            jax.ShapeDtypeStruct((z.nodes, z.width), BF),
            jax.ShapeDtypeStruct((z.spaces, z.width, z.nodes), F32),
        ),
        in_specs=[ANY] * 7 + [VMEM] * (z.spaces - 1),
        out_specs=[VMEM] * 5,
        scratch_shapes=[
            pltpu.SMEM((z.tiles,), jnp.int32),
            pltpu.SMEM((z.tiles,), jnp.int32),
            pltpu.VMEM((1, z.nodes), jnp.int32),
            pltpu.VMEM((z.width, z.width), BF),
            pltpu.VMEM((2 * z.width, z.width), BF),
            pltpu.VMEM((z.tiles, z.rows, z.rows), BF),
            pltpu.VMEM((z.spaces * z.blocks, z.rows, z.width), BF),
            pltpu.VMEM((z.blocks, z.rows, z.width), F32),
            pltpu.VMEM((z.slots, z.nodes), BF),
            pltpu.VMEM((z.nodes, z.width), BF),
            pltpu.SemaphoreType.DMA((6 + CHUNKS,)),
        ],
        cost_estimate=pl.CostEstimate(
            flops=4400000000, bytes_accessed=1000, transcendentals=0
        ),
        compiler_params=pltpu.CompilerParams(vmem_limit_bytes=24 << 20),
        name="forward",
    )


def backward_call(z):
    lanes = 2 * z.half * z.nodes
    low = z.width // 2

    def kernel(recv_hbm, send_hbm, kern_hbm, w_msg_hbm, w_node_hbm, lat_hbm, returned, slot,
               factor, agg, pre_slope, *rest):
        others, rest = rest[: z.spaces - 1], rest[z.spaces - 1 :]
        payload, keep, grad_keep, direct = rest[:4]
        recv, send, w_msg, w_node, kern, place, back, spread, latent, sems = rest[4:]
        lats = (latent, *others)
        copies = [
            pltpu.make_async_copy(src, dst, sems.at[i])
            for i, (src, dst) in enumerate(
                [
                    (w_node_hbm, w_node),
                    (recv_hbm, recv),
                    (send_hbm, send),
                    (w_msg_hbm, w_msg),
                    (lat_hbm, latent),
                ]
            )
        ]
        copies += z.tile_copies(kern_hbm, kern, sems, len(copies))
        for copy in copies:
            copy.start()
        slot_row = slot[...].astype(jnp.int32)
        for at in range(0, z.slots, 128):
            down = iota((128, z.nodes), 0) + at
            place[at : at + 128, :] = (down == slot_row).astype(F32).astype(BF)
        returned_t = jnp.transpose(returned[...].astype(F32)).astype(BF)
        incoming_t = mm(returned_t, place[...])
        slope_t = (incoming_t * factor[...]).astype(BF)
        copies[0].wait()
        rows_t = mm(w_node[...], slope_t)
        direct[...] = rows_t[: z.width] + incoming_t
        back_t = rows_t[z.width :].astype(BF)
        for block in range(z.blocks):
            back[block] = back_t[:, block * z.rows : (block + 1) * z.rows]
        spread[...] = jnp.zeros_like(spread)
        copies[1].wait()
        copies[2].wait()

        def spread_tile(t):
            s = z.place_of(send[t])
            spread[s] = spread[s] + mm(back[recv[t]], kern[t])

        z.each_tile(spread_tile, copies[5:])
        copies[3].wait()
        copies[4].wait()

        joined = jnp.concatenate([lats[0][...], agg[...]], axis=1)
        grad_node = mm(slope_t, joined)
        grad_msg = jnp.zeros((z.width, z.width), F32)
        for step in range(z.half):
            for other in range(2):
                part = 2 * ((-step) % z.half) + other
                total = jnp.concatenate(
                    [spread[part * z.blocks + block] for block in range(z.blocks)], axis=1
                )
                preact_grad = (total * pre_slope[part]).astype(BF)
                grad_msg += mm(preact_grad, lats[part][...])
                back_lat = mm(w_msg[...], preact_grad)
                if other:
                    at = step * z.nodes
                    payload[:, at : at + z.nodes] = back_lat[:low].astype(BF)
                    at += z.half * z.nodes
                    payload[:, at : at + z.nodes] = back_lat[low:].astype(BF)
                else:
                    keep[step] = back_lat
        grads = jnp.concatenate([grad_msg, grad_node], axis=1)
        first = (lax.axis_index("space") & 1) == 0
        grad_keep[...] = jnp.where(first, grads[:low], grads[low:])
        payload[:, lanes:] = jnp.where(first, grads[low:], grads[:low]).astype(BF)

    return pl.pallas_call(
        kernel,
        out_shape=(
            jax.ShapeDtypeStruct((low, lanes + 3 * z.width), BF),
            jax.ShapeDtypeStruct((z.half, z.width, z.nodes), F32),
            jax.ShapeDtypeStruct((low, 3 * z.width), F32),
            jax.ShapeDtypeStruct((z.width, z.nodes), F32),
        ),
        in_specs=[ANY] * 6 + [VMEM] * (4 + z.spaces),
        out_specs=[VMEM] * 4,
        scratch_shapes=[
            pltpu.SMEM((z.tiles,), jnp.int32),
            pltpu.SMEM((z.tiles,), jnp.int32),
            pltpu.VMEM((z.width, z.width), BF),
            pltpu.VMEM((2 * z.width, z.width), BF),
            pltpu.VMEM((z.tiles, z.rows, z.rows), BF),
            pltpu.VMEM((z.slots, z.nodes), BF),
            pltpu.VMEM((z.blocks, z.width, z.rows), BF),
            pltpu.VMEM((z.spaces * z.blocks, z.width, z.rows), F32),
            pltpu.VMEM((z.nodes, z.width), BF),
            pltpu.SemaphoreType.DMA((5 + CHUNKS,)),
        ],
        cost_estimate=pl.CostEstimate(
            flops=1000000, bytes_accessed=1000, transcendentals=0
        ),
        compiler_params=pltpu.CompilerParams(vmem_limit_bytes=24 << 20),
        name="backward",
    )


def pair_call(z):
    lanes = 2 * z.half * z.nodes
    low = z.width // 2

    def kernel(payload, keep, grad_keep, *outs):
        grad, own, sent = outs[0], outs[1], outs[2:]
        grad[...] = (grad_keep[...] + payload[:, lanes:].astype(F32)).astype(BF)
        for step in range(z.half):
            at = step * z.nodes
            top = payload[:, at : at + z.nodes].astype(F32)
            at += z.half * z.nodes
            bottom = payload[:, at : at + z.nodes].astype(F32)
            total = keep[step] + jnp.concatenate([top, bottom], axis=0)
            if step:
                sent[step - 1][...] = total.astype(BF)
            else:
                own[...] = total

    return pl.pallas_call(
        kernel,
        out_shape=(
            jax.ShapeDtypeStruct((low, 3 * z.width), BF),
            jax.ShapeDtypeStruct((z.width, z.nodes), F32),
            *[jax.ShapeDtypeStruct((z.width, z.nodes), BF)] * (z.half - 1),
        ),
        in_specs=[VMEM] * 3,
        out_specs=[VMEM] * (1 + z.half),
        compiler_params=pltpu.CompilerParams(vmem_limit_bytes=8 << 20),
        name="pair",
    )


def finish_call(z):
    def kernel(direct, own, *rest):
        total = own[...] + direct[...]
        for ref in rest[:-1]:
            total = total + ref[...].astype(F32)
        rest[-1][...] = jnp.transpose(total).astype(BF)

    return pl.pallas_call(
        kernel,
        out_shape=jax.ShapeDtypeStruct((z.nodes, z.width), BF),
        in_specs=[VMEM] * (1 + z.half),
        compiler_params=pltpu.CompilerParams(vmem_limit_bytes=8 << 20),
        name="finish",
    )


def weights_call(z):
    def kernel(mine, other, grad_msg, grad_node):
        first = (lax.axis_index("space") & 1) == 0
        mine, other = mine[...], other[...]
        total = jnp.concatenate(
            [jnp.where(first, mine, other), jnp.where(first, other, mine)], axis=0
        )
        grad_msg[...] = jnp.transpose(total[:, : z.width])
        grad_node[...] = jnp.transpose(total[:, z.width :])

    return pl.pallas_call(
        kernel,
        out_shape=(
            jax.ShapeDtypeStruct((z.width, z.width), F32),
            jax.ShapeDtypeStruct((2 * z.width, z.width), F32),
        ),
        in_specs=[VMEM] * 2,
        compiler_params=pltpu.CompilerParams(vmem_limit_bytes=8 << 20),
        name="weights",
    )


def emit_call(z):
    def kernel(rows, out, sem):
        copy = pltpu.make_async_copy(rows, out, sem)
        copy.start()
        copy.wait()

    return pl.pallas_call(
        kernel,
        out_shape=jax.ShapeDtypeStruct((z.slots, z.width), BF),
        in_specs=[VMEM],
        out_specs=ANY,
        scratch_shapes=[pltpu.SemaphoreType.DMA],
        compiler_params=pltpu.CompilerParams(vmem_limit_bytes=8 << 20),
        name="emit",
    )


def body(latent, owner_ids, tile_recv, tile_send, kernels, w_msg, w_node, upstream):
    z = Sizes(latent, kernels, upstream)
    devices = z.groups * z.spaces

    def swap(value):
        return lax.all_to_all(
            value.reshape(z.groups, z.capacity, z.width),
            "group", split_axis=0, concat_axis=0, tiled=True,
        ).reshape(z.slots, z.width)

    def to_core(value):
        return lax.ppermute(value, "space", [(i, i ^ 1) for i in range(z.spaces)])

    def along(value, step):
        return lax.ppermute(
            value, "space", [(i, (i + 2 * step) % z.spaces) for i in range(z.spaces)]
        )

    def flip(value, mask):
        return lax.ppermute(value, ("group", "space"), [(i, i ^ mask) for i in range(devices)])

    far = [along(latent, step) for step in range(1, z.half)]
    near = to_core(lax.optimization_barrier((latent, *far))[0])
    lats = [near]
    for part in far:
        lats += [part, to_core(part)]
    returned = swap(upstream)
    params = [in_hbm(one) for one in (tile_recv, tile_send, kernels, w_msg, w_node, latent)]
    owners = in_hbm(owner_ids.reshape(1, z.nodes))
    outgoing, slot, factor, agg, pre_slope = forward_call(z)(
        params[0], params[1], owners, *params[2:], *lats
    )
    updated = swap(outgoing)
    payload, keep, grad_keep, direct = backward_call(z)(
        *params, returned, slot, factor, agg, pre_slope, *lats
    )
    grad, own, *sent = pair_call(z)(to_core(payload), keep, grad_keep)

    got = [along(part, step + 1) for step, part in enumerate(sent)]
    latent_grad = finish_call(z)(direct, own, *got)

    bits = devices.bit_length() - 1
    for at in reversed(range(1, bits, 2)):
        span = min(2, bits - at)
        grad = grad.astype(BF)
        got = [grad] + [flip(grad, step << at) for step in range(1, 1 << span)]
        if at == 1:
            got[-1], latent_grad = lax.optimization_barrier((got[-1], latent_grad))
        got = [one.astype(F32) for one in got]
        grad = got[0] + got[1]
        if span == 2:
            grad = grad + (got[2] + got[3])
    grad_msg, grad_node = weights_call(z)(grad, to_core(grad))
    grad_msg, updated = lax.optimization_barrier((grad_msg, updated))
    updated = emit_call(z)(updated)
    return updated, latent_grad, grad_msg, grad_node


def solution(mesh):
    split = P(("group", "space"))
    wide = P(("group", "space"), None)
    return jax.shard_map(
        body,
        mesh=mesh,
        in_specs=(wide, wide, split, split, P(("group", "space"), None, None), P(), P(), wide),
        out_specs=(wide, wide, P(), P()),
        check_vma=False,
    )
```

```python
import jax
import jax.numpy as jnp
from jax import lax
from jax.experimental import pallas as pl
from jax.experimental.pallas import tpu as pltpu
from jax.sharding import PartitionSpec as P

BF = jnp.bfloat16
CHUNKS = 2
F32 = jnp.float32
VMEM = pl.BlockSpec(memory_space=pltpu.VMEM)
ANY = pl.BlockSpec(memory_space=pltpu.HBM)


def mm(left, right):
    return jnp.dot(left, right, preferred_element_type=F32)


def mm_nt(left, right):
    return lax.dot_general(left, right, (((1,), (1,)), ((), ())), preferred_element_type=F32)


def sigmoid(value):
    return 0.5 * jnp.tanh(0.5 * value) + 0.5


def slope_of(value):
    sig = sigmoid(value)
    return sig * (1.0 + value * (1.0 - sig))


def in_hbm(value):
    return pltpu.with_memory_space_constraint(value, pltpu.HBM)


def iota(shape, axis):
    return lax.broadcasted_iota(jnp.int32, shape, axis)


class Sizes:
    def __init__(self, latent, kernels, upstream):
        self.nodes, self.width = latent.shape
        self.tiles, self.rows, _ = kernels.shape
        self.groups, self.spaces = lax.axis_size("group"), lax.axis_size("space")
        self.slots = upstream.shape[0]
        self.capacity = self.slots // self.groups
        self.blocks = self.nodes // self.rows
        self.half = self.spaces // 2
        self.chunk = self.tiles // CHUNKS
        self.hot = max(16, -(-self.groups // 16) * 16)

    def tile_copies(self, kern_hbm, kern, sems, first):
        return [
            pltpu.make_async_copy(
                kern_hbm.at[pl.ds(i * self.chunk, self.chunk)],
                kern.at[pl.ds(i * self.chunk, self.chunk)],
                sems.at[first + i],
            )
            for i in range(CHUNKS)
        ]

    def each_tile(self, step, copies):
        for i, copy in enumerate(copies):
            copy.wait()
            for t in range(i * self.chunk, (i + 1) * self.chunk):
                step(t)

    def place_of(self, sender):
        me = lax.axis_index("space")
        device = sender // self.blocks
        step = lax.rem((me >> 1) - (device >> 1) + self.half, self.half)
        other = (me & 1) ^ (device & 1)
        return (2 * step + other) * self.blocks + lax.rem(sender, self.blocks)


def forward_call(z):
    def kernel(recv_hbm, send_hbm, owner_hbm, kern_hbm, w_msg_hbm, w_node_hbm, lat_hbm, *rest):
        others, rest = rest[: z.spaces - 1], rest[z.spaces - 1 :]
        outgoing, slot_out, factor, agg, pre_slope = rest[:5]
        recv, send, owner, w_msg, w_node, kern, msg, acc, place, latent, sems = rest[5:]
        lats = (latent, *others)
        copies = [
            pltpu.make_async_copy(src, dst, sems.at[i])
            for i, (src, dst) in enumerate(
                [
                    (owner_hbm, owner),
                    (w_msg_hbm, w_msg),
                    (lat_hbm, latent),
                    (recv_hbm, recv),
                    (send_hbm, send),
                    (w_node_hbm, w_node),
                ]
            )
        ]
        copies += z.tile_copies(kern_hbm, kern, sems, len(copies))
        for copy in copies:
            copy.start()
        copies[0].wait()

        owner_row = owner[...]
        hot = (iota((z.hot, z.nodes), 0) == owner_row).astype(F32)
        before = (iota((z.nodes, z.nodes), 0) < iota((z.nodes, z.nodes), 1)).astype(F32)
        counts = mm(hot.astype(BF), before.astype(BF))
        rank = jnp.sum(counts * hot, axis=0, keepdims=True)
        slot = owner_row.astype(F32) * z.capacity + rank
        slot_row = slot.astype(jnp.int32)
        slot_out[...] = slot
        for at in range(0, z.slots, 128):
            down = iota((128, z.nodes), 0) + at
            place[at : at + 128, :] = (down == slot_row).astype(F32).astype(BF)

        copies[1].wait()
        copies[2].wait()
        for part in range(z.spaces):
            preact = mm(lats[part][...], w_msg[...])
            value = (preact * sigmoid(preact)).astype(BF)
            for block in range(z.blocks):
                msg[part * z.blocks + block] = value[block * z.rows : (block + 1) * z.rows, :]

        for copy in copies[3:6]:
            copy.wait()
        acc[...] = jnp.zeros_like(acc)

        def gather_tile(t):
            r = recv[t]
            acc[r] = acc[r] + mm(kern[t], msg[z.place_of(send[t])])

        z.each_tile(gather_tile, copies[6:])
        aggregate = acc[...].reshape(z.nodes, z.width).astype(BF)
        agg[...] = aggregate
        own = latent[...]
        mixed = mm(jnp.concatenate([own, aggregate], axis=1), w_node[...])
        sig = sigmoid(mixed)
        factor[...] = jnp.transpose(sig * (1.0 + mixed * (1.0 - sig)))
        new_rows = (own.astype(F32) + mixed * sig).astype(BF)
        for at in range(0, z.slots, 256):
            outgoing[at : at + 256, :] = mm(place[at : at + 256, :], new_rows).astype(BF)

        w_msg_t = jnp.transpose(w_msg[...].astype(F32)).astype(BF)
        for part in range(z.spaces):
            pre_slope[part] = slope_of(mm_nt(w_msg_t, lats[part][...]))

    return pl.pallas_call(
        kernel,
        out_shape=(
            jax.ShapeDtypeStruct((z.slots, z.width), BF),
            jax.ShapeDtypeStruct((1, z.nodes), F32),
            jax.ShapeDtypeStruct((z.width, z.nodes), F32),
            jax.ShapeDtypeStruct((z.nodes, z.width), BF),
            jax.ShapeDtypeStruct((z.spaces, z.width, z.nodes), F32),
        ),
        in_specs=[ANY] * 7 + [VMEM] * (z.spaces - 1),
        out_specs=[VMEM] * 5,
        scratch_shapes=[
            pltpu.SMEM((z.tiles,), jnp.int32),
            pltpu.SMEM((z.tiles,), jnp.int32),
            pltpu.VMEM((1, z.nodes), jnp.int32),
            pltpu.VMEM((z.width, z.width), BF),
            pltpu.VMEM((2 * z.width, z.width), BF),
            pltpu.VMEM((z.tiles, z.rows, z.rows), BF),
            pltpu.VMEM((z.spaces * z.blocks, z.rows, z.width), BF),
            pltpu.VMEM((z.blocks, z.rows, z.width), F32),
            pltpu.VMEM((z.slots, z.nodes), BF),
            pltpu.VMEM((z.nodes, z.width), BF),
            pltpu.SemaphoreType.DMA((6 + CHUNKS,)),
        ],
        cost_estimate=pl.CostEstimate(
            flops=4400000000, bytes_accessed=1000, transcendentals=0
        ),
        compiler_params=pltpu.CompilerParams(vmem_limit_bytes=24 << 20),
        name="forward",
    )


def backward_call(z):
    lanes = 2 * z.half * z.nodes
    low = z.width // 2

    def kernel(recv_hbm, send_hbm, kern_hbm, w_msg_hbm, w_node_hbm, lat_hbm, returned, slot,
               factor, agg, pre_slope, *rest):
        others, rest = rest[: z.spaces - 1], rest[z.spaces - 1 :]
        payload, keep, grad_send, grad_keep, direct = rest[:5]
        recv, send, w_msg, w_node, kern, place, back, spread, latent, sems = rest[5:]
        lats = (latent, *others)
        copies = [
            pltpu.make_async_copy(src, dst, sems.at[i])
            for i, (src, dst) in enumerate(
                [
                    (w_node_hbm, w_node),
                    (recv_hbm, recv),
                    (send_hbm, send),
                    (w_msg_hbm, w_msg),
                    (lat_hbm, latent),
                ]
            )
        ]
        copies += z.tile_copies(kern_hbm, kern, sems, len(copies))
        for copy in copies:
            copy.start()
        slot_row = slot[...].astype(jnp.int32)
        for at in range(0, z.slots, 128):
            down = iota((128, z.nodes), 0) + at
            place[at : at + 128, :] = (down == slot_row).astype(F32).astype(BF)
        returned_t = jnp.transpose(returned[...].astype(F32)).astype(BF)
        incoming_t = mm(returned_t, place[...])
        slope_t = (incoming_t * factor[...]).astype(BF)
        copies[0].wait()
        rows_t = mm(w_node[...], slope_t)
        direct[...] = rows_t[: z.width] + incoming_t
        back_t = rows_t[z.width :].astype(BF)
        for block in range(z.blocks):
            back[block] = back_t[:, block * z.rows : (block + 1) * z.rows]
        spread[...] = jnp.zeros_like(spread)
        copies[1].wait()
        copies[2].wait()

        def spread_tile(t):
            s = z.place_of(send[t])
            spread[s] = spread[s] + mm(back[recv[t]], kern[t])

        z.each_tile(spread_tile, copies[5:])
        copies[3].wait()
        copies[4].wait()

        joined = jnp.concatenate([lats[0][...], agg[...]], axis=1)
        grad_node = mm(slope_t, joined)
        grad_msg = jnp.zeros((z.width, z.width), F32)
        for step in range(z.half):
            for other in range(2):
                part = 2 * ((-step) % z.half) + other
                total = jnp.concatenate(
                    [spread[part * z.blocks + block] for block in range(z.blocks)], axis=1
                )
                preact_grad = (total * pre_slope[part]).astype(BF)
                grad_msg += mm(preact_grad, lats[part][...])
                back_lat = mm(w_msg[...], preact_grad)
                if other:
                    at = step * z.nodes
                    payload[:, at : at + z.nodes] = back_lat[:low].astype(BF)
                    at += z.half * z.nodes
                    payload[:, at : at + z.nodes] = back_lat[low:].astype(BF)
                else:
                    keep[step] = back_lat
        grads = jnp.concatenate([grad_msg, grad_node], axis=1)
        first = (lax.axis_index("space") & 1) == 0
        grad_keep[...] = jnp.where(first, grads[:low], grads[low:])
        grad_send[...] = jnp.where(first, grads[low:], grads[:low]).astype(BF)

    return pl.pallas_call(
        kernel,
        out_shape=(
            jax.ShapeDtypeStruct((low, lanes), BF),
            jax.ShapeDtypeStruct((z.half, z.width, z.nodes), F32),
            jax.ShapeDtypeStruct((low, 3 * z.width), BF),
            jax.ShapeDtypeStruct((low, 3 * z.width), F32),
            jax.ShapeDtypeStruct((z.width, z.nodes), F32),
        ),
        in_specs=[ANY] * 6 + [VMEM] * (4 + z.spaces),
        out_specs=[VMEM] * 5,
        scratch_shapes=[
            pltpu.SMEM((z.tiles,), jnp.int32),
            pltpu.SMEM((z.tiles,), jnp.int32),
            pltpu.VMEM((z.width, z.width), BF),
            pltpu.VMEM((2 * z.width, z.width), BF),
            pltpu.VMEM((z.tiles, z.rows, z.rows), BF),
            pltpu.VMEM((z.slots, z.nodes), BF),
            pltpu.VMEM((z.blocks, z.width, z.rows), BF),
            pltpu.VMEM((z.spaces * z.blocks, z.width, z.rows), F32),
            pltpu.VMEM((z.nodes, z.width), BF),
            pltpu.SemaphoreType.DMA((5 + CHUNKS,)),
        ],
        cost_estimate=pl.CostEstimate(
            flops=1000000, bytes_accessed=1000, transcendentals=0
        ),
        compiler_params=pltpu.CompilerParams(vmem_limit_bytes=24 << 20),
        name="backward",
    )


def pair_call(z):
    def kernel(payload, keep, own, *sent):
        for step in range(z.half):
            at = step * z.nodes
            top = payload[:, at : at + z.nodes].astype(F32)
            at += z.half * z.nodes
            bottom = payload[:, at : at + z.nodes].astype(F32)
            total = keep[step] + jnp.concatenate([top, bottom], axis=0)
            if step:
                sent[step - 1][...] = total.astype(BF)
            else:
                own[...] = total

    return pl.pallas_call(
        kernel,
        out_shape=(
            jax.ShapeDtypeStruct((z.width, z.nodes), F32),
            *[jax.ShapeDtypeStruct((z.width, z.nodes), BF)] * (z.half - 1),
        ),
        in_specs=[VMEM] * 2,
        out_specs=[VMEM] * z.half,
        compiler_params=pltpu.CompilerParams(vmem_limit_bytes=8 << 20),
        name="pair",
    )


def finish_call(z):
    def kernel(direct, own, *rest):
        total = own[...] + direct[...]
        for ref in rest[:-1]:
            total = total + ref[...].astype(F32)
        rest[-1][...] = jnp.transpose(total).astype(BF)

    return pl.pallas_call(
        kernel,
        out_shape=jax.ShapeDtypeStruct((z.nodes, z.width), BF),
        in_specs=[VMEM] * (1 + z.half),
        compiler_params=pltpu.CompilerParams(vmem_limit_bytes=8 << 20),
        name="finish",
    )


def weights_call(z):
    def kernel(mine, other, grad_msg, grad_node):
        first = (lax.axis_index("space") & 1) == 0
        mine, other = mine[...], other[...]
        total = jnp.concatenate(
            [jnp.where(first, mine, other), jnp.where(first, other, mine)], axis=0
        )
        grad_msg[...] = jnp.transpose(total[:, : z.width])
        grad_node[...] = jnp.transpose(total[:, z.width :])

    return pl.pallas_call(
        kernel,
        out_shape=(
            jax.ShapeDtypeStruct((z.width, z.width), F32),
            jax.ShapeDtypeStruct((2 * z.width, z.width), F32),
        ),
        in_specs=[VMEM] * 2,
        compiler_params=pltpu.CompilerParams(vmem_limit_bytes=8 << 20),
        name="weights",
    )


def emit_call(z):
    def kernel(rows, out, sem):
        copy = pltpu.make_async_copy(rows, out, sem)
        copy.start()
        copy.wait()

    return pl.pallas_call(
        kernel,
        out_shape=jax.ShapeDtypeStruct((z.slots, z.width), BF),
        in_specs=[VMEM],
        out_specs=ANY,
        scratch_shapes=[pltpu.SemaphoreType.DMA],
        compiler_params=pltpu.CompilerParams(vmem_limit_bytes=8 << 20),
        name="emit",
    )


def body(latent, owner_ids, tile_recv, tile_send, kernels, w_msg, w_node, upstream):
    z = Sizes(latent, kernels, upstream)
    devices = z.groups * z.spaces

    def swap(value):
        return lax.all_to_all(
            value.reshape(z.groups, z.capacity, z.width),
            "group", split_axis=0, concat_axis=0, tiled=True,
        ).reshape(z.slots, z.width)

    def to_core(value):
        return lax.ppermute(value, "space", [(i, i ^ 1) for i in range(z.spaces)])

    def along(value, step):
        return lax.ppermute(
            value, "space", [(i, (i + 2 * step) % z.spaces) for i in range(z.spaces)]
        )

    def flip(value, mask):
        return lax.ppermute(value, ("group", "space"), [(i, i ^ mask) for i in range(devices)])

    far = [along(latent, step) for step in range(1, z.half)]
    near = to_core(lax.optimization_barrier((latent, *far))[0])
    lats = [near]
    for part in far:
        lats += [part, to_core(part)]
    returned = swap(upstream)
    params = [in_hbm(one) for one in (tile_recv, tile_send, kernels, w_msg, w_node, latent)]
    owners = in_hbm(owner_ids.reshape(1, z.nodes))
    outgoing, slot, factor, agg, pre_slope = forward_call(z)(
        params[0], params[1], owners, *params[2:], *lats
    )
    updated = swap(outgoing)
    payload, keep, grad_send, grad_keep, direct = backward_call(z)(
        *params, returned, slot, factor, agg, pre_slope, *lats
    )
    grad = grad_keep + to_core(grad_send).astype(F32)
    own, *sent = pair_call(z)(to_core(payload), keep)

    got = [along(part, step + 1) for step, part in enumerate(sent)]
    latent_grad = finish_call(z)(direct, own, *got)

    bits = devices.bit_length() - 1
    for at in reversed(range(1, bits, 2)):
        span = min(2, bits - at)
        grad = grad.astype(BF)
        got = [grad] + [flip(grad, step << at) for step in range(1, 1 << span)]
        if at == 1:
            got[-1], latent_grad = lax.optimization_barrier((got[-1], latent_grad))
        got = [one.astype(F32) for one in got]
        grad = got[0] + got[1]
        if span == 2:
            grad = grad + (got[2] + got[3])
    grad_msg, grad_node = weights_call(z)(grad, to_core(grad))
    grad_msg, updated = lax.optimization_barrier((grad_msg, updated))
    updated = emit_call(z)(updated)
    return updated, latent_grad, grad_msg, grad_node


def solution(mesh):
    split = P(("group", "space"))
    wide = P(("group", "space"), None)
    return jax.shard_map(
        body,
        mesh=mesh,
        in_specs=(wide, wide, split, split, P(("group", "space"), None, None), P(), P(), wide),
        out_specs=(wide, wide, P(), P()),
        check_vma=False,
    )
```

```python
import jax
import jax.numpy as jnp
from jax import lax
from jax.experimental import pallas as pl
from jax.experimental.pallas import tpu as pltpu
from jax.sharding import PartitionSpec as P

BF = jnp.bfloat16
CHUNKS = 2
F32 = jnp.float32
VMEM = pl.BlockSpec(memory_space=pltpu.VMEM)
ANY = pl.BlockSpec(memory_space=pltpu.HBM)


def mm(left, right):
    return jnp.dot(left, right, preferred_element_type=F32)


def mm_nt(left, right):
    return lax.dot_general(left, right, (((1,), (1,)), ((), ())), preferred_element_type=F32)


def sigmoid(value):
    return 0.5 * jnp.tanh(0.5 * value) + 0.5


def slope_of(value):
    sig = sigmoid(value)
    return sig * (1.0 + value * (1.0 - sig))


def in_hbm(value):
    return pltpu.with_memory_space_constraint(value, pltpu.HBM)


def iota(shape, axis):
    return lax.broadcasted_iota(jnp.int32, shape, axis)


class Sizes:
    def __init__(self, latent, kernels, upstream):
        self.nodes, self.width = latent.shape
        self.tiles, self.rows, _ = kernels.shape
        self.groups, self.spaces = lax.axis_size("group"), lax.axis_size("space")
        self.slots = upstream.shape[0]
        self.capacity = self.slots // self.groups
        self.blocks = self.nodes // self.rows
        self.half = self.spaces // 2
        self.chunk = self.tiles // CHUNKS
        self.hot = max(16, -(-self.groups // 16) * 16)

    def tile_copies(self, kern_hbm, kern, sems, first):
        return [
            pltpu.make_async_copy(
                kern_hbm.at[pl.ds(i * self.chunk, self.chunk)],
                kern.at[pl.ds(i * self.chunk, self.chunk)],
                sems.at[first + i],
            )
            for i in range(CHUNKS)
        ]

    def each_tile(self, step, copies):
        for i, copy in enumerate(copies):
            copy.wait()
            for t in range(i * self.chunk, (i + 1) * self.chunk):
                step(t)

    def place_of(self, sender):
        me = lax.axis_index("space")
        device = sender // self.blocks
        step = lax.rem((me >> 1) - (device >> 1) + self.half, self.half)
        other = (me & 1) ^ (device & 1)
        return (2 * step + other) * self.blocks + lax.rem(sender, self.blocks)


def forward_call(z):
    def kernel(recv_hbm, send_hbm, owner_hbm, kern_hbm, w_msg_hbm, w_node_hbm, lat_hbm, *rest):
        others, rest = rest[: z.spaces - 1], rest[z.spaces - 1 :]
        outgoing, slot_out, factor, agg, pre_slope = rest[:5]
        recv, send, owner, w_msg, w_node, kern, msg, acc, place, latent, sems = rest[5:]
        lats = (latent, *others)
        copies = [
            pltpu.make_async_copy(src, dst, sems.at[i])
            for i, (src, dst) in enumerate(
                [
                    (owner_hbm, owner),
                    (w_msg_hbm, w_msg),
                    (lat_hbm, latent),
                    (recv_hbm, recv),
                    (send_hbm, send),
                    (w_node_hbm, w_node),
                ]
            )
        ]
        copies += z.tile_copies(kern_hbm, kern, sems, len(copies))
        for copy in copies:
            copy.start()
        copies[0].wait()

        owner_row = owner[...]
        hot = (iota((z.hot, z.nodes), 0) == owner_row).astype(F32)
        before = (iota((z.nodes, z.nodes), 0) < iota((z.nodes, z.nodes), 1)).astype(F32)
        counts = mm(hot.astype(BF), before.astype(BF))
        rank = jnp.sum(counts * hot, axis=0, keepdims=True)
        slot = owner_row.astype(F32) * z.capacity + rank
        slot_row = slot.astype(jnp.int32)
        slot_out[...] = slot
        for at in range(0, z.slots, 128):
            down = iota((128, z.nodes), 0) + at
            place[at : at + 128, :] = (down == slot_row).astype(F32).astype(BF)

        copies[1].wait()
        copies[2].wait()
        for part in range(z.spaces):
            preact = mm(lats[part][...], w_msg[...])
            value = (preact * sigmoid(preact)).astype(BF)
            for block in range(z.blocks):
                msg[part * z.blocks + block] = value[block * z.rows : (block + 1) * z.rows, :]

        for copy in copies[3:6]:
            copy.wait()
        acc[...] = jnp.zeros_like(acc)

        def gather_tile(t):
            r = recv[t]
            acc[r] = acc[r] + mm(kern[t], msg[z.place_of(send[t])])

        z.each_tile(gather_tile, copies[6:])
        aggregate = acc[...].reshape(z.nodes, z.width).astype(BF)
        agg[...] = aggregate
        own = latent[...]
        mixed = mm(jnp.concatenate([own, aggregate], axis=1), w_node[...])
        sig = sigmoid(mixed)
        factor[...] = jnp.transpose(sig * (1.0 + mixed * (1.0 - sig)))
        new_rows = (own.astype(F32) + mixed * sig).astype(BF)
        for at in range(0, z.slots, 256):
            outgoing[at : at + 256, :] = mm(place[at : at + 256, :], new_rows).astype(BF)

        w_msg_t = jnp.transpose(w_msg[...].astype(F32)).astype(BF)
        for part in range(z.spaces):
            pre_slope[part] = slope_of(mm_nt(w_msg_t, lats[part][...]))

    return pl.pallas_call(
        kernel,
        out_shape=(
            jax.ShapeDtypeStruct((z.slots, z.width), BF),
            jax.ShapeDtypeStruct((1, z.nodes), F32),
            jax.ShapeDtypeStruct((z.width, z.nodes), F32),
            jax.ShapeDtypeStruct((z.nodes, z.width), BF),
            jax.ShapeDtypeStruct((z.spaces, z.width, z.nodes), F32),
        ),
        in_specs=[ANY] * 7 + [VMEM] * (z.spaces - 1),
        out_specs=[VMEM] * 5,
        scratch_shapes=[
            pltpu.SMEM((z.tiles,), jnp.int32),
            pltpu.SMEM((z.tiles,), jnp.int32),
            pltpu.VMEM((1, z.nodes), jnp.int32),
            pltpu.VMEM((z.width, z.width), BF),
            pltpu.VMEM((2 * z.width, z.width), BF),
            pltpu.VMEM((z.tiles, z.rows, z.rows), BF),
            pltpu.VMEM((z.spaces * z.blocks, z.rows, z.width), BF),
            pltpu.VMEM((z.blocks, z.rows, z.width), F32),
            pltpu.VMEM((z.slots, z.nodes), BF),
            pltpu.VMEM((z.nodes, z.width), BF),
            pltpu.SemaphoreType.DMA((6 + CHUNKS,)),
        ],
        cost_estimate=pl.CostEstimate(
            flops=4400000000, bytes_accessed=1000, transcendentals=0
        ),
        compiler_params=pltpu.CompilerParams(vmem_limit_bytes=24 << 20),
        name="forward",
    )


def backward_call(z):
    lanes = 2 * z.half * z.nodes
    low = z.width // 2

    def kernel(recv_hbm, send_hbm, kern_hbm, w_msg_hbm, w_node_hbm, lat_hbm, returned, slot,
               factor, agg, pre_slope, *rest):
        others, rest = rest[: z.spaces - 1], rest[z.spaces - 1 :]
        payload, keep, grad_send, grad_keep, direct = rest[:5]
        recv, send, w_msg, w_node, kern, place, back, spread, latent, sems = rest[5:]
        lats = (latent, *others)
        copies = [
            pltpu.make_async_copy(src, dst, sems.at[i])
            for i, (src, dst) in enumerate(
                [
                    (w_node_hbm, w_node),
                    (recv_hbm, recv),
                    (send_hbm, send),
                    (w_msg_hbm, w_msg),
                    (lat_hbm, latent),
                ]
            )
        ]
        copies += z.tile_copies(kern_hbm, kern, sems, len(copies))
        for copy in copies:
            copy.start()
        slot_row = slot[...].astype(jnp.int32)
        for at in range(0, z.slots, 128):
            down = iota((128, z.nodes), 0) + at
            place[at : at + 128, :] = (down == slot_row).astype(F32).astype(BF)
        returned_t = jnp.transpose(returned[...].astype(F32)).astype(BF)
        incoming_t = mm(returned_t, place[...])
        slope_t = (incoming_t * factor[...]).astype(BF)
        copies[0].wait()
        rows_t = mm(w_node[...], slope_t)
        direct[...] = rows_t[: z.width] + incoming_t
        back_t = rows_t[z.width :].astype(BF)
        for block in range(z.blocks):
            back[block] = back_t[:, block * z.rows : (block + 1) * z.rows]
        spread[...] = jnp.zeros_like(spread)
        copies[1].wait()
        copies[2].wait()

        def spread_tile(t):
            s = z.place_of(send[t])
            spread[s] = spread[s] + mm(back[recv[t]], kern[t])

        z.each_tile(spread_tile, copies[5:])
        copies[3].wait()
        copies[4].wait()

        joined = jnp.concatenate([lats[0][...], agg[...]], axis=1)
        grad_node = mm(slope_t, joined)
        grad_msg = jnp.zeros((z.width, z.width), F32)
        for step in range(z.half):
            for other in range(2):
                part = 2 * ((-step) % z.half) + other
                total = jnp.concatenate(
                    [spread[part * z.blocks + block] for block in range(z.blocks)], axis=1
                )
                preact_grad = (total * pre_slope[part]).astype(BF)
                grad_msg += mm(preact_grad, lats[part][...])
                back_lat = mm(w_msg[...], preact_grad)
                if other:
                    at = step * z.nodes
                    payload[:, at : at + z.nodes] = back_lat[:low].astype(BF)
                    at += z.half * z.nodes
                    payload[:, at : at + z.nodes] = back_lat[low:].astype(BF)
                else:
                    keep[step] = back_lat
        grads = jnp.concatenate([grad_msg, grad_node], axis=1)
        first = (lax.axis_index("space") & 1) == 0
        grad_keep[...] = jnp.where(first, grads[:low], grads[low:])
        grad_send[...] = jnp.where(first, grads[low:], grads[:low]).astype(BF)

    return pl.pallas_call(
        kernel,
        out_shape=(
            jax.ShapeDtypeStruct((low, lanes), BF),
            jax.ShapeDtypeStruct((z.half, z.width, z.nodes), F32),
            jax.ShapeDtypeStruct((low, 3 * z.width), BF),
            jax.ShapeDtypeStruct((low, 3 * z.width), F32),
            jax.ShapeDtypeStruct((z.width, z.nodes), F32),
        ),
        in_specs=[ANY] * 6 + [VMEM] * (4 + z.spaces),
        out_specs=[VMEM] * 5,
        scratch_shapes=[
            pltpu.SMEM((z.tiles,), jnp.int32),
            pltpu.SMEM((z.tiles,), jnp.int32),
            pltpu.VMEM((z.width, z.width), BF),
            pltpu.VMEM((2 * z.width, z.width), BF),
            pltpu.VMEM((z.tiles, z.rows, z.rows), BF),
            pltpu.VMEM((z.slots, z.nodes), BF),
            pltpu.VMEM((z.blocks, z.width, z.rows), BF),
            pltpu.VMEM((z.spaces * z.blocks, z.width, z.rows), F32),
            pltpu.VMEM((z.nodes, z.width), BF),
            pltpu.SemaphoreType.DMA((5 + CHUNKS,)),
        ],
        cost_estimate=pl.CostEstimate(
            flops=1000000, bytes_accessed=1000, transcendentals=0
        ),
        compiler_params=pltpu.CompilerParams(vmem_limit_bytes=24 << 20),
        name="backward",
    )


def pair_call(z):
    def kernel(payload, keep, own, *sent):
        for step in range(z.half):
            at = step * z.nodes
            top = payload[:, at : at + z.nodes].astype(F32)
            at += z.half * z.nodes
            bottom = payload[:, at : at + z.nodes].astype(F32)
            total = keep[step] + jnp.concatenate([top, bottom], axis=0)
            if step:
                sent[step - 1][...] = total.astype(BF)
            else:
                own[...] = total

    return pl.pallas_call(
        kernel,
        out_shape=(
            jax.ShapeDtypeStruct((z.width, z.nodes), F32),
            *[jax.ShapeDtypeStruct((z.width, z.nodes), BF)] * (z.half - 1),
        ),
        in_specs=[VMEM] * 2,
        out_specs=[VMEM] * z.half,
        compiler_params=pltpu.CompilerParams(vmem_limit_bytes=8 << 20),
        name="pair",
    )


def finish_call(z):
    def kernel(direct, own, *rest):
        total = own[...] + direct[...]
        for ref in rest[:-1]:
            total = total + ref[...].astype(F32)
        rest[-1][...] = jnp.transpose(total).astype(BF)

    return pl.pallas_call(
        kernel,
        out_shape=jax.ShapeDtypeStruct((z.nodes, z.width), BF),
        in_specs=[VMEM] * (1 + z.half),
        compiler_params=pltpu.CompilerParams(vmem_limit_bytes=8 << 20),
        name="finish",
    )


def weights_call(z):
    def kernel(mine, other, updated, grad_msg, grad_node, updated_out, sem):
        copy = pltpu.make_async_copy(updated, updated_out, sem)
        copy.start()
        first = (lax.axis_index("space") & 1) == 0
        mine, other = mine[...], other[...]
        total = jnp.concatenate(
            [jnp.where(first, mine, other), jnp.where(first, other, mine)], axis=0
        )
        grad_msg[...] = jnp.transpose(total[:, : z.width])
        grad_node[...] = jnp.transpose(total[:, z.width :])
        copy.wait()

    return pl.pallas_call(
        kernel,
        out_shape=(
            jax.ShapeDtypeStruct((z.width, z.width), F32),
            jax.ShapeDtypeStruct((2 * z.width, z.width), F32),
            jax.ShapeDtypeStruct((z.slots, z.width), BF),
        ),
        in_specs=[VMEM] * 3,
        out_specs=[pl.BlockSpec(), pl.BlockSpec(), ANY],
        scratch_shapes=[pltpu.SemaphoreType.DMA],
        compiler_params=pltpu.CompilerParams(vmem_limit_bytes=8 << 20),
        name="weights",
    )


def body(latent, owner_ids, tile_recv, tile_send, kernels, w_msg, w_node, upstream):
    z = Sizes(latent, kernels, upstream)
    devices = z.groups * z.spaces

    def swap(value):
        return lax.all_to_all(
            value.reshape(z.groups, z.capacity, z.width),
            "group", split_axis=0, concat_axis=0, tiled=True,
        ).reshape(z.slots, z.width)

    def to_core(value):
        return lax.ppermute(value, "space", [(i, i ^ 1) for i in range(z.spaces)])

    def along(value, step):
        return lax.ppermute(
            value, "space", [(i, (i + 2 * step) % z.spaces) for i in range(z.spaces)]
        )

    def flip(value, mask):
        return lax.ppermute(value, ("group", "space"), [(i, i ^ mask) for i in range(devices)])

    far = [along(latent, step) for step in range(1, z.half)]
    near = to_core(lax.optimization_barrier((latent, *far))[0])
    lats = [near]
    for part in far:
        lats += [part, to_core(part)]
    returned = swap(upstream)
    params = [in_hbm(one) for one in (tile_recv, tile_send, kernels, w_msg, w_node, latent)]
    owners = in_hbm(owner_ids.reshape(1, z.nodes))
    outgoing, slot, factor, agg, pre_slope = forward_call(z)(
        params[0], params[1], owners, *params[2:], *lats
    )
    updated = swap(outgoing)
    payload, keep, grad_send, grad_keep, direct = backward_call(z)(
        *params, returned, slot, factor, agg, pre_slope, *lats
    )
    grad = grad_keep + to_core(grad_send).astype(F32)
    own, *sent = pair_call(z)(to_core(payload), keep)

    got = [along(part, step + 1) for step, part in enumerate(sent)]
    latent_grad = finish_call(z)(direct, own, *got)

    bits = devices.bit_length() - 1
    for at in reversed(range(1, bits, 2)):
        span = min(2, bits - at)
        grad = grad.astype(BF)
        got = [grad] + [flip(grad, step << at) for step in range(1, 1 << span)]
        if at == 1:
            got[-1], latent_grad = lax.optimization_barrier((got[-1], latent_grad))
        got = [one.astype(F32) for one in got]
        grad = got[0] + got[1]
        if span == 2:
            grad = grad + (got[2] + got[3])
    grad_msg, grad_node, updated = weights_call(z)(grad, to_core(grad), updated)
    return updated, latent_grad, grad_msg, grad_node


def solution(mesh):
    split = P(("group", "space"))
    wide = P(("group", "space"), None)
    return jax.shard_map(
        body,
        mesh=mesh,
        in_specs=(wide, wide, split, split, P(("group", "space"), None, None), P(), P(), wide),
        out_specs=(wide, wide, P(), P()),
        check_vma=False,
    )
```
